256 devices in a mesh: seq: 32 (over x, z), tp: 4 (over y), lat: 2 (over core).
Axes of the slice: x: 4, y: 4, z: 8, core: 2. Of those that a mesh axis runs over, the one named last changes fastest.
Arguments:
- tokens: bfloat16 [24576, 8192], P(('seq', 'lat'), 'tp'), may hold values from -6 to 6
- active: int32 [24576, 4], P(('seq', 'lat')), may hold values from 0 to 255, all different within a row; in each aligned block of 384 rows (0 to 383, 384 to 767, ...) at most 9 rows name the same one
- placement_map: int32 [256], replicated, may hold values from 0 to 255, each once
- enc_weight: bfloat16 [8192, 32768], P('tp', ('seq', 'lat')), may hold values from -0.0625 to 0.0625
- enc_bias: float32 [32768], P(('seq', 'lat')), may hold values from -3 to 3
- dec_weight: bfloat16 [32768, 8192], P(('seq', 'lat'), 'tp'), may hold values from -0.375 to 0.375
- dec_bias: float32 [8192], P('tp'), may hold values from -3 to 3
Outputs:
- recon: bfloat16 [24576, 8192], P(('seq', 'lat'), 'tp')
The draws below stay inside these ranges and needn't reach their ends.
Inputs may be any that keep to these rules, and one draw needn't show every extreme that they name: `active`: the 4 blocks of one token are different. Among the rows of one device (aligned blocks of 384 rows) no block is named more than 9 times, and some block is named exactly 9 times. `placement_map`: each column block appears once.
All inputs are finite; a program needn't handle non-finite values.
Results may differ from the reference program's by a relative error of at most 0.0061.
Values may be sent and summed in bfloat16 or wider, within the bound.
A program may use at most 128 MiB of HBM per device.

```python
import math
import jax
import jax.numpy as jnp
import numpy as np
from jax import lax

D = 8192
BLKW = 128
K = 4
TOK_DEV = 384
NBLK = 256
LATENTS = 32768
TOKENS = 24576
CAP = 9
N_SEQ = 32
N_LAT = 2


def steps_of(key, extent, split, least, largest):
    def one(dim, parts):
        heights = jax.random.uniform(jax.random.fold_in(jax.random.fold_in(key, 6), dim), (parts,), jnp.float32, least / len(split), largest / len(split))
        return jnp.repeat(jnp.exp(heights), extent[dim] // parts).reshape((-1,) + (1,) * (len(extent) - dim - 1))

    loudness = one(*split[0])
    for cut in split[1:]:
        loudness = loudness * one(*cut)
    return loudness


def assign_block(rng, own, number, rows, number_of, top, reach, lean):
    ranking = jax.random.permutation(rng, number_of)
    crowded, usual = portions_of(number_of, rows * top, reach, lean, True), portions_of(number_of, rows * top, reach, lean, False)
    places = jnp.arange(number_of)

    def named(tallies, turn):
        used = int((tallies > 0).sum())
        fixed = max(1, used // 4)
        passed = fixed + (places - fixed + turn * (used - fixed)) % max(1, number_of - fixed)
        return jnp.zeros((number_of,), jnp.int32).at[ranking[jnp.where(places < fixed, places, passed)]].set(jnp.asarray(tallies, jnp.int32))

    tallies = jnp.where(number % 4 == 0, named(crowded, number // 4), named(usual, number - number // 4 - 1))
    mixed = jax.random.permutation(jax.random.fold_in(own, 3), number_of)
    giver, sink = mixed[0:number_of // 2 * 2:2], mixed[1:number_of // 2 * 2:2]
    room = jnp.minimum(tallies[giver] - 1, reach - tallies[sink]) // 2
    room = jnp.where((giver == ranking[0]) | (sink == ranking[0]) | (tallies[sink] == 0), 0, jnp.maximum(room, 0))
    passed = jax.random.randint(jax.random.fold_in(own, 4), (number_of // 2,), 0, 1 << 20) % (room + 1)
    tallies = tallies.at[giver].add(-passed).at[sink].add(passed)
    labels = jnp.searchsorted(jnp.cumsum(tallies), jnp.arange(rows * top), side="right").astype(jnp.int32)
    table = labels.reshape(top, rows).T
    table = table[jax.random.permutation(jax.random.fold_in(own, 1), rows)]
    turn = jax.random.randint(jax.random.fold_in(own, 2), (rows, 1), 0, top)
    return jnp.take_along_axis(table, (jnp.arange(top)[None, :] + turn) % top, axis=1)


def portions_of(count, total, reach, slope, full):
    loads = [(1 << 20) // math.isqrt(grade ** slope) + 1 for grade in range(1, count + 1)]
    largest = reach if full else min(reach, max(-(-total // count), total * loads[0] // sum(loads)))
    least = 1 if total - largest >= count - 1 else 0
    counts, spare = [largest] + [least] * (count - 1), total - largest - least * (count - 1)
    while spare > 0:
        candidates = [i for i in range(1, count) if counts[i] < largest] or [i for i in range(1, count) if counts[i] < reach]
        whole, budget = sum([loads[i] for i in candidates]), spare
        for i in candidates:
            extra = min(reach - counts[i], max(1, budget * loads[i] // whole), spare)
            counts[i] = counts[i] + extra
            spare = spare - extra
    return np.array(counts)


def bell_draw(rng, extent, deviation, reach, split=(), kind=jnp.bfloat16):
    entries = jax.random.normal(rng, extent, jnp.float32) * deviation
    if len(split) > 0:
        entries = steps_of(rng, extent, split, -0.22, 0.18) * entries
    return jnp.clip(entries, min=-reach, max=reach).astype(kind)


def setup_inputs(seed: int = 0) -> dict:
    seeds = jax.random.split(jax.random.key(seed), 8)
    tokens = bell_draw(seeds[0], (TOKENS, D), 1.0, 6.0, ((0, 64), (1, 4)))
    active_keys = jax.random.split(jax.random.fold_in(seeds[1], 1), TOKENS // TOK_DEV)
    active_turns = jax.random.permutation(jax.random.fold_in(seeds[1], 3), TOKENS // TOK_DEV)
    active = jax.vmap(lambda own, number: assign_block(jax.random.fold_in(seeds[1], 2), own, number, TOK_DEV, NBLK, K, CAP, 2))(active_keys, active_turns).reshape((TOKENS, K))
    placement_map = jax.random.permutation(seeds[2], NBLK).astype(jnp.int32)
    enc_weight = bell_draw(seeds[3], (D, LATENTS), D ** -0.5, 0.0625, ((0, 4), (1, 64)))
    enc_bias = bell_draw(seeds[4], (LATENTS,), 0.5, 3.0, ((0, 64),), jnp.float32)
    dec_weight = bell_draw(seeds[5], (LATENTS, D), (K * BLKW // 2) ** -0.5, 0.375, ((0, 64), (1, 4)))
    dec_bias = bell_draw(seeds[6], (D,), 0.5, 3.0, ((0, 4),), jnp.float32)
    return {"tokens": tokens, "active": active, "placement_map": placement_map, "enc_weight": enc_weight, "enc_bias": enc_bias, "dec_weight": dec_weight, "dec_bias": dec_bias}


def reference(tokens, active, placement_map, enc_weight, enc_bias, dec_weight, dec_bias):
    centered = (tokens.astype(jnp.float32) - dec_bias[None, :]).astype(jnp.bfloat16)
    padded = jnp.concatenate([centered, jnp.zeros((1, D), jnp.bfloat16)], axis=0)
    position = placement_map[active].astype(jnp.int32)
    flat = position.reshape(-1)
    pair_row = (jnp.arange(TOKENS * K, dtype=jnp.int32) // K).astype(jnp.int32)
    hot = (flat[:, None] == jnp.arange(NBLK, dtype=jnp.int32)[None, :]).astype(jnp.int32)
    rank = jnp.sum((jnp.cumsum(hot, axis=0) - 1) * hot, axis=1).astype(jnp.int32)
    depth = N_SEQ * N_LAT * CAP
    table = jnp.full((NBLK, depth), TOKENS, jnp.int32).at[flat, rank].set(pair_row)

    def one_block(total, block):
        index = table[block]
        gathered = padded[index]
        start = (block * BLKW).astype(jnp.int32)
        w_enc = lax.dynamic_slice_in_dim(enc_weight, start, BLKW, 1)
        b_enc = lax.dynamic_slice_in_dim(enc_bias, start, BLKW, 0)
        preact = jnp.dot(gathered, w_enc, preferred_element_type=jnp.float32) + b_enc[None, :]
        codes = jnp.maximum(preact, 0.0).astype(jnp.bfloat16)
        w_dec = lax.dynamic_slice_in_dim(dec_weight, start, BLKW, 0)
        part = jnp.dot(codes, w_dec, preferred_element_type=jnp.float32).astype(jnp.bfloat16)
        total = total.at[index].add(part.astype(jnp.float32))
        return total, None

    total = jnp.zeros((TOKENS + 1, D), jnp.float32)
    total, _ = lax.scan(one_block, total, jnp.arange(NBLK, dtype=jnp.int32))
    return (total[:TOKENS] + dec_bias[None, :]).astype(jnp.bfloat16)
```

```python
import jax
import jax.numpy as jnp
from jax import lax
from jax.experimental import pallas as pl
from jax.experimental.pallas import tpu as pltpu
from jax.sharding import PartitionSpec as P

NX, NZ = 4, 8
PAD = 16
MESH = pl.DeviceIdType.MESH
BF, F32 = jnp.bfloat16, jnp.float32


def kernel(tokens, act, table, enc, bias, dec, dbias, out, tokbuf,
           enc_all, dec_all, bias_all, tgt, stage, last, work, picks, preact, parts_in, codes,
           rs_first, rs_in,
           tok_s, tok_r, tgt_s, tgt_r, w_s, w_r, ys_s, ys_r, yc_s, yc_r, rs_s, rs_r, loc):
    rows, width = tokens.shape
    half = rows // 2
    blocks = table.shape[0]
    row_blocks = blocks // NZ
    slots = row_blocks * PAD
    quarter = slots // 4
    s, y, c = lax.axis_index("seq"), lax.axis_index("tp"), lax.axis_index("lat")
    x, z = s // NZ, s % NZ

    def at(dx=0, dz=0, dy=0, dc=0):
        return (((x + dx + NX) % NX) * NZ + (z + dz + NZ) % NZ, (y + dy) % 4, (c + dc) % 2)

    def member(dx=0, dc=0):
        return ((x + dx + NX) % NX) * 2 + (c + dc) % 2

    def send(src, dst, ss, rs, dev):
        copy = pltpu.make_async_remote_copy(src_ref=src, dst_ref=dst, send_sem=ss, recv_sem=rs,
                                            device_id=dev, device_id_type=MESH)
        copy.start()
        return copy

    sent = []
    peers = [at(dz=1), at(dz=-1), at(dx=1), at(dx=-1), at(dc=1), at(dy=1), at(dy=2), at(dy=3)]
    barrier = pltpu.get_barrier_semaphore()
    for dev in peers:
        pl.semaphore_signal(barrier, inc=1, device_id=dev, device_id_type=MESH)
    pl.semaphore_wait(barrier, len(peers))

    def part(ref, h):
        return ref.at[pl.ds(h * half, half)]

    tok = {}

    def tok_send(d, k, o):
        h = o if d == 0 else 1 - o
        src = tokens if k == 0 else tokbuf.at[2 * k - 2 + d]
        dst = last if k == 3 else tokbuf.at[2 * k + d]
        tok[d, k, o] = send(part(src, h), part(dst, h), tok_s.at[d, k, o], tok_r.at[d, k, o],
                            at(dz=1 if d == 0 else -1))
        sent.append(tok[d, k, o])

    tg = {}

    def tgt_send(d, k):
        src = 0 if k == 0 else 2 * k - 1 + d
        dst = 7 if k == 3 else 2 * k + 1 + d
        tg[d, k] = send(tgt.at[src], tgt.at[dst], tgt_s.at[d, k], tgt_r.at[d, k], at(dz=1 if d == 0 else -1))
        sent.append(tg[d, k])

    wc = {}
    store = (enc_all, dec_all, bias_all)
    own = (enc, dec, bias)

    def w_send(kind, slot, m, dev, first=False, piece=None):
        dst = store[kind].at[m]
        src = own[kind] if first else dst
        if piece is not None:
            n = src.shape[0] // 2
            src, dst = src.at[pl.ds(piece * n, n)], dst.at[pl.ds(piece * n, n)]
        wc[kind, slot] = send(src, dst, w_s.at[kind, slot], w_r.at[kind, slot], dev)
        sent.append(wc[kind, slot])

    def w_start(kind):
        w_send(kind, 0, member(), at(dx=1), first=True)
        w_send(kind, 1, member(), at(dx=-1), first=True)
        w_send(kind, 2, member(), at(dc=1), first=True)

    def w_second(kind):
        wc[kind, 0].wait_recv()
        if kind == 2:
            w_send(kind, 3, member(-1), at(dx=1))
        else:
            w_send(kind, 3, member(-1), at(dx=1), piece=0)
        wc[kind, 1].wait_recv()
        if kind != 2:
            w_send(kind, 4, member(1), at(dx=-1), piece=1)
        w_send(kind, 5, member(-1), at(dc=1))
        w_send(kind, 6, member(1), at(dc=1))

    def w_third(kind):
        wc[kind, 3].wait_recv()
        if kind != 2:
            wc[kind, 4].wait_recv()
        w_send(kind, 7, member(2), at(dc=1))

    def w_done(kind):
        for slot in (2, 5, 6, 7):
            wc[kind, slot].wait_recv()

    tok_send(0, 0, 0)
    tok_send(1, 0, 0)
    tok_send(0, 0, 1)
    tok_send(1, 0, 1)
    w_start(2)
    w_start(0)
    local = [pltpu.make_async_copy(tokens, stage, loc.at[0]),
             pltpu.make_async_copy(enc, enc_all.at[member()], loc.at[1]),
             pltpu.make_async_copy(dec, dec_all.at[member()], loc.at[2]),
             pltpu.make_async_copy(bias, bias_all.at[member()], loc.at[3])]
    for copy in local:
        copy.start()

    ids = lax.broadcasted_iota(jnp.int32, (blocks, rows), 0)
    hits = [act[pl.ds(k, 1), :] == ids for k in range(4)]
    named = (hits[0] | hits[1]) | (hits[2] | hits[3])
    before = (lax.broadcasted_iota(jnp.int32, (rows, rows), 0)
              < lax.broadcasted_iota(jnp.int32, (rows, rows), 1))
    rank = jnp.dot(jnp.where(named, 1.0, 0.0).astype(BF), jnp.where(before, 1.0, 0.0).astype(BF),
                   preferred_element_type=F32)
    where_to = rank + table[...]
    for k in range(4):
        tgt[0, pl.ds(k, 1), :] = jnp.sum(jnp.where(hits[k], where_to, 0.0), axis=0, keepdims=True)
    tgt[0, pl.ds(4, 4), :] = jnp.full((4, rows), -1.0, F32)
    tgt_send(0, 0)
    tgt_send(1, 0)

    base = (z * slots).astype(F32)

    def encode(ref, i):
        def pick(j, carry):
            n = slots // 4
            r0 = pl.multiple_of(j * n, n)
            place = (lax.broadcasted_iota(jnp.int32, (n, rows), 0) + r0).astype(F32) + base
            t = tgt[i]
            hit = ((t[0:1] == place) | (t[1:2] == place)) | ((t[2:3] == place) | (t[3:4] == place))
            picks[pl.ds(r0, n), :] = jnp.where(hit, 1.0, 0.0).astype(BF)
            return carry

        lax.fori_loop(0, 4, pick, 0)

        def gather(j, carry):
            n = width // 4
            c0 = pl.multiple_of(j * n, n)
            got = jnp.dot(picks[...], ref[:, pl.ds(c0, n)], preferred_element_type=F32)
            work[0, :, pl.ds(c0, n)] = (got - dbias[:, pl.ds(c0, n)]).astype(BF)
            return carry

        lax.fori_loop(0, 4, gather, 0)

        def one(m, carry):
            for b in range(4):
                r0 = pl.multiple_of((m * 4 + b) * PAD, PAD)
                preact[i, pl.ds(r0, PAD), :] = jnp.dot(
                    work[0, pl.ds(r0, PAD), :], enc_all[m, :, pl.ds(b * 128, 128)], preferred_element_type=F32)
            return carry

        lax.fori_loop(0, 8, one, 0)

    ysum, ycode = {}, {}

    def y_start(g, i, n):
        for o in range(1, 4):
            to = pl.multiple_of(((y + o) % 4) * quarter, quarter)
            ysum[g, o] = send(preact.at[pl.ds(i, n), pl.ds(to, quarter)], parts_in.at[o - 1, pl.ds(i, n)],
                              ys_s.at[g, o - 1], ys_r.at[g, o - 1], at(dy=o))
            sent.append(ysum[g, o])

    mine = pl.multiple_of(y * quarter, quarter)

    def y_codes(g, i, n):
        for o in range(1, 4):
            ysum[g, o].wait_recv()
        per = bias_all[pl.ds(2 * y, 2)].reshape(quarter // PAD, 1, 128)
        for j in range(i, i + n):
            total = preact[j, pl.ds(mine, quarter), :] + parts_in[0, j] + parts_in[1, j] + parts_in[2, j]
            total = total.reshape(quarter // PAD, PAD, 128) + per
            codes[j, pl.ds(mine, quarter), :] = jnp.maximum(total, 0.0).astype(BF).reshape(quarter, 128)
        for o in range(1, 4):
            view = codes.at[pl.ds(i, n), pl.ds(mine, quarter)]
            ycode[g, o] = send(view, view, yc_s.at[g, o - 1], yc_r.at[g, o - 1], at(dy=o))
            sent.append(ycode[g, o])

    def y_done(g):
        for o in range(1, 4):
            ycode[g, o].wait_recv()

    def tok_pass(k, o):
        for d in range(2):
            tok[d, k, o].wait_recv()
            if k < 2 or o == 0:
                tok_send(d, k + 1, o)

    def tgt_pass(k):
        for d in range(2):
            tg[d, k].wait_recv()
            if k < 2 or d == 0:
                tgt_send(d, k + 1)

    def staged(g):
        def step(j, carry):
            i = 2 * g - 1 + j
            copy = pltpu.make_async_copy(tokbuf.at[i - 1], stage, loc.at[4])
            copy.start()
            copy.wait()
            encode(stage, i)
            return carry

        lax.fori_loop(0, 2, step, 0)
        y_start(g, 2 * g - 1, 2)

    tgt_pass(0)
    tok_pass(0, 0)
    w_second(2)
    w_third(2)
    tok_pass(0, 1)
    tgt_pass(1)
    w_second(0)
    w_start(1)
    tok_pass(1, 0)
    tgt_pass(2)
    for copy in local:
        copy.wait()
    tok_pass(1, 1)
    w_third(0)
    w_done(2)
    w_done(0)
    encode(stage, 0)
    y_start(0, 0, 1)
    staged(1)
    y_codes(0, 0, 1)
    tok_pass(2, 0)
    staged(2)
    y_codes(1, 1, 2)
    w_second(1)
    tok_pass(2, 1)
    staged(3)
    y_codes(2, 3, 2)
    tg[0, 3].wait_recv()
    tok[0, 3, 0].wait_recv()
    tok[1, 3, 0].wait_recv()
    encode(last, 7)
    y_start(4, 7, 1)
    y_codes(3, 5, 2)
    w_third(1)
    y_codes(4, 7, 1)
    w_done(1)
    for g in range(5):
        y_done(g)

    def decode(i, buf):
        def one(m, carry):
            for b in range(4):
                r0 = pl.multiple_of((m * 4 + b) * PAD, PAD)
                work[buf, pl.ds(r0, PAD), :] = jnp.dot(
                    codes[i, pl.ds(r0, PAD), :], dec_all[m, pl.ds(b * 128, 128), :],
                    preferred_element_type=F32).astype(BF)
            return carry

        lax.fori_loop(0, 8, one, 0)

    def spread(i, h):
        t = jnp.concatenate([tgt[i], jnp.zeros((120, rows), F32)], axis=0)
        cols = jnp.transpose(t)[h * half:(h + 1) * half]
        place = lax.broadcasted_iota(jnp.int32, (half, slots), 1).astype(F32) + base
        hit = (((cols[:, 0:1] == place) | (cols[:, 1:2] == place))
               | ((cols[:, 2:3] == place) | (cols[:, 3:4] == place)))
        return jnp.where(hit, 1.0, 0.0).astype(BF)

    def combine(i, buf, h, dst, plus=()):
        sel = spread(i, h)
        for j in range(4):
            n = width // 4
            cs = pl.ds(j * n, n)
            total = jnp.dot(sel, work[buf, :, cs], preferred_element_type=F32)
            for ref in plus:
                total = total + ref[:, cs].astype(F32)
            dst[:, cs] = total.astype(BF)

    rs = {}

    def rs_send(d, k, o, src):
        rs[d, k, o] = send(src, rs_in.at[d, k, o], rs_s.at[d, k, o], rs_r.at[d, k, o],
                           at(dz=1 if d == 0 else -1))
        sent.append(rs[d, k, o])

    decode(7, 0)
    for d in range(2):
        combine(7, 0, d, rs_first.at[d, 0])
        rs_send(d, 0, 0, rs_first.at[d, 0])
    for k in range(1, 4):
        idx = (8 - 2 * k, 7 - 2 * k)
        for d in range(2):
            decode(idx[d], d)
        if k == 1:
            for d in range(2):
                combine(idx[d], d, 1 - d, rs_first.at[d, 1])
                rs_send(d, 1, 1, rs_first.at[d, 1])
        for o in range(2):
            if k == 1 and o == 1:
                continue
            for d in range(2):
                got = rs_in.at[d, k - 1, o]
                rs[d, k - 1, o].wait_recv()
                combine(idx[d], d, o if d == 0 else 1 - o, got, (got,))
                rs_send(d, k, o, got)
    decode(0, 0)
    for o in range(2):
        rs[0, 3, o].wait_recv()
        rs[1, 3, 1 - o].wait_recv()
        combine(0, 0, o, out.at[pl.ds(o * half, half)], (rs_in.at[0, 3, o], rs_in.at[1, 3, 1 - o], dbias))
    for copy in sent:
        copy.wait_send()


def local(tokens, active, placement_map, enc_weight, enc_bias, dec_weight, dec_bias):
    rows, width = tokens.shape
    blocks = placement_map.shape[0]
    slots = blocks // NZ * PAD
    depth = enc_weight.shape[1]
    p = placement_map
    table = ((p // 8) % NZ * slots + (p // (8 * NZ) * 8 + p % 8) * PAD).astype(F32).reshape(blocks, 1)
    vmem, hbm = pl.BlockSpec(memory_space=pltpu.VMEM), pl.BlockSpec(memory_space=pl.ANY)
    half = rows // 2
    dma = pltpu.SemaphoreType.DMA
    out, _ = pl.pallas_call(
        kernel,
        out_shape=(jax.ShapeDtypeStruct((rows, width), BF), jax.ShapeDtypeStruct((6, rows, width), BF)),
        in_specs=[hbm, vmem, vmem, hbm, vmem, hbm, vmem],
        out_specs=(vmem, hbm),
        scratch_shapes=[
            pltpu.VMEM((8, width, depth), BF),
            pltpu.VMEM((8, depth, width), BF),
            pltpu.VMEM((8, 4, 128), F32),
            pltpu.VMEM((8, 8, rows), F32),
            pltpu.VMEM((rows, width), BF),
            pltpu.VMEM((rows, width), BF),
            pltpu.VMEM((2, slots, width), BF),
            pltpu.VMEM((slots, rows), BF),
            pltpu.VMEM((8, slots, 128), F32),
            pltpu.VMEM((3, 8, slots // 4, 128), F32),
            pltpu.VMEM((8, slots, 128), BF),
            pltpu.VMEM((2, 2, half, width), BF),
            pltpu.VMEM((2, 4, 2, half, width), BF),
            dma((2, 4, 2)), dma((2, 4, 2)),
            dma((2, 4)), dma((2, 4)),
            dma((3, 8)), dma((3, 8)),
            dma((5, 3)), dma((5, 3)),
            dma((5, 3)), dma((5, 3)),
            dma((2, 4, 2)), dma((2, 4, 2)),
            dma((5,)),
        ],
        compiler_params=pltpu.CompilerParams(collective_id=0, has_side_effects=True, vmem_limit_bytes=63 << 20),
        name="encode_decode",
    )(tokens, active.T, table, enc_weight, enc_bias.reshape(4, 128), dec_weight, dec_bias.reshape(1, width))
    return out


def solution(mesh):
    return jax.shard_map(
        local,
        mesh=mesh,
        in_specs=(
            P(("seq", "lat"), "tp"),
            P(("seq", "lat"), None),
            P(),
            P("tp", ("seq", "lat")),
            P(("seq", "lat")),
            P(("seq", "lat"), "tp"),
            P("tp"),
        ),
        out_specs=P(("seq", "lat"), "tp"),
        check_vma=False,
    )
```

```python
import jax
import jax.numpy as jnp
from jax import lax
from jax.experimental import pallas as pl
from jax.experimental.pallas import tpu as pltpu
from jax.sharding import PartitionSpec as P

NX, NZ = 4, 8
PAD = 16
MESH = pl.DeviceIdType.MESH
BF, F32 = jnp.bfloat16, jnp.float32


def kernel(tokens, act, table, enc, bias, dec, dbias, out, tokbuf,
           enc_all, dec_all, bias_all, tgt, stage, last, work, picks, preact, parts_in, codes, sels,
           rs_first, rs_in,
           tok_s, tok_r, tgt_s, tgt_r, w_s, w_r, ys_s, ys_r, yc_s, yc_r, rs_s, rs_r, loc):
    rows, width = tokens.shape
    half = rows // 2
    blocks = table.shape[0]
    row_blocks = blocks // NZ
    slots = row_blocks * PAD
    quarter = slots // 4
    s, y, c = lax.axis_index("seq"), lax.axis_index("tp"), lax.axis_index("lat")
    x, z = s // NZ, s % NZ

    def at(dx=0, dz=0, dy=0, dc=0):
        return (((x + dx + NX) % NX) * NZ + (z + dz + NZ) % NZ, (y + dy) % 4, (c + dc) % 2)

    def member(dx=0, dc=0):
        return ((x + dx + NX) % NX) * 2 + (c + dc) % 2

    def send(src, dst, ss, rs, dev):
        copy = pltpu.make_async_remote_copy(src_ref=src, dst_ref=dst, send_sem=ss, recv_sem=rs,
                                            device_id=dev, device_id_type=MESH)
        copy.start()
        return copy

    sent = []
    peers = [at(dz=1), at(dz=-1), at(dx=1), at(dx=-1), at(dc=1), at(dy=1), at(dy=2), at(dy=3)]
    barrier = pltpu.get_barrier_semaphore()
    for dev in peers:
        pl.semaphore_signal(barrier, inc=1, device_id=dev, device_id_type=MESH)
    pl.semaphore_wait(barrier, len(peers))

    def part(ref, h):
        return ref.at[pl.ds(h * half, half)]

    tok = {}

    def tok_send(d, k, o):
        h = o if d == 0 else 1 - o
        src = tokens if k == 0 else tokbuf.at[2 * k - 2 + d]
        dst = last if k == 3 else tokbuf.at[2 * k + d]
        tok[d, k, o] = send(part(src, h), part(dst, h), tok_s.at[d, k, o], tok_r.at[d, k, o],
                            at(dz=1 if d == 0 else -1))
        sent.append(tok[d, k, o])

    tg = {}

    def tgt_send(d, k):
        src = 0 if k == 0 else 2 * k - 1 + d
        dst = 7 if k == 3 else 2 * k + 1 + d
        tg[d, k] = send(tgt.at[src], tgt.at[dst], tgt_s.at[d, k], tgt_r.at[d, k], at(dz=1 if d == 0 else -1))
        sent.append(tg[d, k])

    wc = {}
    store = (enc_all, dec_all, bias_all)
    own = (enc, dec, bias)

    def w_send(kind, slot, m, dev, first=False, piece=None):
        dst = store[kind].at[m]
        src = own[kind] if first else dst
        if piece is not None:
            n = src.shape[0] // 2
            src, dst = src.at[pl.ds(piece * n, n)], dst.at[pl.ds(piece * n, n)]
        wc[kind, slot] = send(src, dst, w_s.at[kind, slot], w_r.at[kind, slot], dev)
        sent.append(wc[kind, slot])

    def w_first(kind):
        for p in range(2):
            w_send(kind, p, member(), at(dx=1), first=True, piece=p)
            w_send(kind, 3 - p, member(), at(dx=-1), first=True, piece=1 - p)
        w_send(kind, 6, member(), at(dc=1), first=True)

    def w_pass(kind):
        wc[kind, 0].wait_recv()
        w_send(kind, 4, member(-1), at(dx=1), piece=0)
        wc[kind, 3].wait_recv()
        w_send(kind, 5, member(1), at(dx=-1), piece=1)

    def w_mid(kind):
        wc[kind, 1].wait_recv()
        w_send(kind, 7, member(-1), at(dc=1))
        wc[kind, 2].wait_recv()
        w_send(kind, 8, member(1), at(dc=1))

    def w_last(kind):
        for p in range(2):
            wc[kind, 4 + p].wait_recv()
            w_send(kind, 9 + p, member(2), at(dc=1), piece=p)

    def w_done(kind, slots):
        for slot in slots:
            wc[kind, slot].wait_recv()

    def b_first():
        w_send(2, 0, member(), at(dx=1), first=True)
        w_send(2, 1, member(), at(dx=-1), first=True)
        w_send(2, 6, member(), at(dc=1), first=True)

    def b_pass():
        wc[2, 0].wait_recv()
        w_send(2, 4, member(-1), at(dx=1))
        w_send(2, 7, member(-1), at(dc=1))
        wc[2, 1].wait_recv()
        w_send(2, 8, member(1), at(dc=1))

    def b_last():
        wc[2, 4].wait_recv()
        w_send(2, 9, member(2), at(dc=1))

    tok_send(0, 0, 0)
    tok_send(1, 0, 0)
    tok_send(0, 0, 1)
    tok_send(1, 0, 1)
    b_first()
    w_first(0)
    local = [pltpu.make_async_copy(tokens, stage, loc.at[0]),
             pltpu.make_async_copy(enc, enc_all.at[member()], loc.at[1]),
             pltpu.make_async_copy(dec, dec_all.at[member()], loc.at[2]),
             pltpu.make_async_copy(bias, bias_all.at[member()], loc.at[3])]
    for copy in local:
        copy.start()

    ids = lax.broadcasted_iota(jnp.int32, (blocks, rows), 0)
    hits = [act[pl.ds(k, 1), :] == ids for k in range(4)]
    named = (hits[0] | hits[1]) | (hits[2] | hits[3])
    before = (lax.broadcasted_iota(jnp.int32, (rows, rows), 0)
              < lax.broadcasted_iota(jnp.int32, (rows, rows), 1))
    rank = jnp.dot(jnp.where(named, 1.0, 0.0).astype(BF), jnp.where(before, 1.0, 0.0).astype(BF),
                   preferred_element_type=F32)
    where_to = rank + table[...]
    for k in range(4):
        tgt[0, pl.ds(k, 1), :] = jnp.sum(jnp.where(hits[k], where_to, 0.0), axis=0, keepdims=True)
    tgt[0, pl.ds(4, 4), :] = jnp.full((4, rows), -1.0, F32)
    tgt_send(0, 0)
    tgt_send(1, 0)

    base = (z * slots).astype(F32)

    def encode(ref, i):
        def pick(j, carry):
            n = slots // 4
            r0 = pl.multiple_of(j * n, n)
            place = (lax.broadcasted_iota(jnp.int32, (n, rows), 0) + r0).astype(F32) + base
            t = tgt[i]
            hit = ((t[0:1] == place) | (t[1:2] == place)) | ((t[2:3] == place) | (t[3:4] == place))
            picks[pl.ds(r0, n), :] = jnp.where(hit, 1.0, 0.0).astype(BF)
            return carry

        lax.fori_loop(0, 4, pick, 0)

        def gather(j, carry):
            n = width // 4
            c0 = pl.multiple_of(j * n, n)
            got = jnp.dot(picks[...], ref[:, pl.ds(c0, n)], preferred_element_type=F32)
            work[0, :, pl.ds(c0, n)] = (got - dbias[:, pl.ds(c0, n)]).astype(BF)
            return carry

        lax.fori_loop(0, 4, gather, 0)

        def one(m, carry):
            for b in range(4):
                r0 = pl.multiple_of((m * 4 + b) * PAD, PAD)
                preact[i, pl.ds(r0, PAD), :] = jnp.dot(
                    work[0, pl.ds(r0, PAD), :], enc_all[m, :, pl.ds(b * 128, 128)], preferred_element_type=F32)
            return carry

        lax.fori_loop(0, 8, one, 0)

    ysum, ycode = {}, {}

    def y_start(g, i, n):
        for o in range(1, 4):
            to = pl.multiple_of(((y + o) % 4) * quarter, quarter)
            ysum[g, o] = send(preact.at[pl.ds(i, n), pl.ds(to, quarter)], parts_in.at[o - 1, pl.ds(i, n)],
                              ys_s.at[g, o - 1], ys_r.at[g, o - 1], at(dy=o))
            sent.append(ysum[g, o])

    mine = pl.multiple_of(y * quarter, quarter)

    def y_codes(g, i, n):
        for o in range(1, 4):
            ysum[g, o].wait_recv()
        per = bias_all[pl.ds(2 * y, 2)].reshape(quarter // PAD, 1, 128)
        for j in range(i, i + n):
            total = preact[j, pl.ds(mine, quarter), :] + parts_in[0, j] + parts_in[1, j] + parts_in[2, j]
            total = total.reshape(quarter // PAD, PAD, 128) + per
            codes[j, pl.ds(mine, quarter), :] = jnp.maximum(total, 0.0).astype(BF).reshape(quarter, 128)
        for o in range(1, 4):
            view = codes.at[pl.ds(i, n), pl.ds(mine, quarter)]
            ycode[g, o] = send(view, view, yc_s.at[g, o - 1], yc_r.at[g, o - 1], at(dy=o))
            sent.append(ycode[g, o])

    def y_done(g):
        for o in range(1, 4):
            ycode[g, o].wait_recv()

    def tok_pass(k, o):
        for d in range(2):
            tok[d, k, o].wait_recv()
            if k < 2 or o == 0:
                tok_send(d, k + 1, o)

    def tgt_pass(k):
        for d in range(2):
            tg[d, k].wait_recv()
            if k < 2 or d == 0:
                tgt_send(d, k + 1)

    def staged(g):
        def step(j, carry):
            i = 2 * g - 1 + j
            copy = pltpu.make_async_copy(tokbuf.at[i - 1], stage, loc.at[4])
            copy.start()
            copy.wait()
            encode(stage, i)
            return carry

        lax.fori_loop(0, 2, step, 0)
        y_start(g, 2 * g - 1, 2)

    def decode(i, buf, lo=0, hi=8):
        def one(j, carry):
            q = j // 2
            m = ((x + q + q // 2 - 2 * (q // 3)) % NX) * 2 + j % 2
            for b in range(4):
                r0 = pl.multiple_of((m * 4 + b) * PAD, PAD)
                work[buf, pl.ds(r0, PAD), :] = jnp.dot(
                    codes[i, pl.ds(r0, PAD), :], dec_all[m, pl.ds(b * 128, 128), :],
                    preferred_element_type=F32).astype(BF)
            return carry

        lax.fori_loop(lo, hi, one, 0)

    def spread(i, h):
        t = jnp.concatenate([tgt[i], jnp.zeros((120, rows), F32)], axis=0)
        cols = jnp.transpose(t)[h * half:(h + 1) * half]
        place = lax.broadcasted_iota(jnp.int32, (half, slots), 1).astype(F32) + base
        hit = (((cols[:, 0:1] == place) | (cols[:, 1:2] == place))
               | ((cols[:, 2:3] == place) | (cols[:, 3:4] == place)))
        return jnp.where(hit, 1.0, 0.0).astype(BF)

    def sums(h, buf, plus):
        for j in range(4):
            n = width // 4
            cs = pl.ds(j * n, n)
            total = jnp.dot(sels[h], work[buf, :, cs], preferred_element_type=F32)
            for ref in plus:
                total = total + ref[:, cs].astype(F32)
            yield cs, total

    def combine(h, buf, dst, plus=()):
        for cs, total in sums(h, buf, plus):
            dst[:, cs] = total.astype(BF)

    rs = {}

    def rs_send(d, k, o, src):
        rs[d, k, o] = send(src, rs_in.at[d, k, o], rs_s.at[d, k, o], rs_r.at[d, k, o],
                           at(dz=1 if d == 0 else -1))
        if k > 1 or (k == 1 and o == 0):
            sent.append(rs[d, k, o])

    def rs_phase():
        for d in range(2):
            combine(d, 0, rs_first.at[d, 0])
            rs_send(d, 0, 0, rs_first.at[d, 0])
        for k in range(1, 4):
            idx = (8 - 2 * k, 7 - 2 * k)
            for d in range(2):
                decode(idx[d], d)
            if k == 1:
                for d in range(2):
                    sels[1 - d] = spread(idx[d], 1 - d)
                    combine(1 - d, d, rs_first.at[d, 1])
                    rs_send(d, 1, 1, rs_first.at[d, 1])
            for o in range(2):
                if k == 1 and o == 1:
                    continue
                for d in range(2):
                    got = rs_in.at[d, k - 1, o]
                    h = o if d == 0 else 1 - o
                    sels[h] = spread(idx[d], h)
                    rs[d, k - 1, o].wait_recv()
                    combine(h, d, got, (got,))
                    rs_send(d, k, o, got)
        decode(0, 0)
        for d in range(2):
            rs[d, 0, 0].wait_send()
            rs[d, 1, 1].wait_send()
            sels[d] = spread(0, d)
        for d in range(2):
            rs[d, 3, 0].wait_recv()
            for cs, total in sums(d, 0, (rs_in.at[d, 3, 0], dbias)):
                top = total.astype(BF)
                rs_first[0, d, :, cs] = top
                rs_first[1, d, :, cs] = (total - top.astype(F32)).astype(BF)
        for d in range(2):
            h = 1 - d
            rs[d, 3, 1].wait_recv()
            for j in range(4):
                cs = pl.ds(j * (width // 4), width // 4)
                total = rs_first[0, h, :, cs].astype(F32) + rs_first[1, h, :, cs].astype(F32)
                out[pl.ds(h * half, half), cs] = (total + rs_in[d, 3, 1, :, cs].astype(F32)).astype(BF)

    b_pass()
    tok_pass(0, 0)
    w_pass(0)
    w_first(1)
    tok_pass(0, 1)
    tgt_pass(0)
    w_mid(0)
    b_last()
    tok_pass(1, 0)
    for copy in local:
        copy.wait()
    tok_pass(1, 1)
    tgt_pass(1)
    w_last(0)
    w_done(2, (6, 7, 8, 9))
    w_done(0, (6, 7, 8, 9, 10))
    encode(stage, 0)
    y_start(0, 0, 1)
    staged(1)
    tok_pass(2, 0)
    y_codes(0, 0, 1)
    w_pass(1)
    staged(2)
    y_codes(1, 1, 2)
    tok_pass(2, 1)
    tgt_pass(2)
    staged(3)
    y_codes(2, 3, 2)
    w_mid(1)
    tok[0, 3, 0].wait_recv()
    tok[1, 3, 0].wait_recv()
    tg[0, 3].wait_recv()
    encode(last, 7)
    y_start(4, 7, 1)
    y_codes(3, 5, 2)
    for h in range(2):
        sels[h] = spread(7, h)
    y_codes(4, 7, 1)
    for g in range(5):
        y_done(g)
    w_done(1, (6, 7, 8))
    decode(7, 0, 0, 6)
    w_last(1)
    w_done(1, (9, 10))
    decode(7, 0, 6, 8)
    rs_phase()
    for copy in sent:
        copy.wait_send()


def local(tokens, active, placement_map, enc_weight, enc_bias, dec_weight, dec_bias):
    rows, width = tokens.shape
    blocks = placement_map.shape[0]
    slots = blocks // NZ * PAD
    depth = enc_weight.shape[1]
    p = placement_map
    table = ((p // 8) % NZ * slots + (p // (8 * NZ) * 8 + p % 8) * PAD).astype(F32).reshape(blocks, 1)
    vmem, hbm = pl.BlockSpec(memory_space=pltpu.VMEM), pl.BlockSpec(memory_space=pl.ANY)
    half = rows // 2
    dma = pltpu.SemaphoreType.DMA
    out, _ = pl.pallas_call(
        kernel,
        out_shape=(jax.ShapeDtypeStruct((rows, width), BF), jax.ShapeDtypeStruct((6, rows, width), BF)),
        in_specs=[hbm, vmem, vmem, hbm, vmem, hbm, vmem],
        out_specs=(vmem, hbm),
        scratch_shapes=[
            pltpu.VMEM((8, width, depth), BF),
            pltpu.VMEM((8, depth, width), BF),
            pltpu.VMEM((8, 4, 128), F32),
            pltpu.VMEM((8, 8, rows), F32),
            pltpu.VMEM((rows, width), BF),
            pltpu.VMEM((rows, width), BF),
            pltpu.VMEM((2, slots, width), BF),
            pltpu.VMEM((slots, rows), BF),
            pltpu.VMEM((8, slots, 128), F32),
            pltpu.VMEM((3, 8, slots // 4, 128), F32),
            pltpu.VMEM((8, slots, 128), BF),
            pltpu.VMEM((2, half, slots), BF),
            pltpu.VMEM((2, 2, half, width), BF),
            pltpu.VMEM((2, 4, 2, half, width), BF),
            dma((2, 4, 2)), dma((2, 4, 2)),
            dma((2, 4)), dma((2, 4)),
            dma((3, 11)), dma((3, 11)),
            dma((5, 3)), dma((5, 3)),
            dma((5, 3)), dma((5, 3)),
            dma((2, 4, 2)), dma((2, 4, 2)),
            dma((5,)),
        ],
        compiler_params=pltpu.CompilerParams(collective_id=0, has_side_effects=True, vmem_limit_bytes=63 << 20),
        name="encode_decode",
    )(tokens, active.T, table, enc_weight, enc_bias.reshape(4, 128), dec_weight, dec_bias.reshape(1, width))
    return out


def solution(mesh):
    return jax.shard_map(
        local,
        mesh=mesh,
        in_specs=(
            P(("seq", "lat"), "tp"),
            P(("seq", "lat"), None),
            P(),
            P("tp", ("seq", "lat")),
            P(("seq", "lat")),
            P(("seq", "lat"), "tp"),
            P("tp"),
        ),
        out_specs=P(("seq", "lat"), "tp"),
        check_vma=False,
    )
```

```python
import jax
import jax.numpy as jnp
from jax import lax
from jax.experimental import pallas as pl
from jax.experimental.pallas import tpu as pltpu
from jax.sharding import PartitionSpec as P

NX, NZ = 4, 8
PAD = 16
MESH = pl.DeviceIdType.MESH
BF, F32 = jnp.bfloat16, jnp.float32


def kernel(tokens, act, table, enc, bias, dec, dbias, out, tokbuf,
           enc_all, dec_all, bias_all, tgt, stage, last, work, picks, preact, parts_in, codes, sels,
           rs_first, rs_in,
           tok_s, tok_r, tgt_s, tgt_r, w_s, w_r, ys_s, ys_r, yc_s, yc_r, rs_s, rs_r, loc):
    rows, width = tokens.shape
    half = rows // 2
    blocks = table.shape[0]
    row_blocks = blocks // NZ
    slots = row_blocks * PAD
    quarter = slots // 4
    s, y, c = lax.axis_index("seq"), lax.axis_index("tp"), lax.axis_index("lat")
    x, z = s // NZ, s % NZ

    def at(dx=0, dz=0, dy=0, dc=0):
        return (((x + dx + NX) % NX) * NZ + (z + dz + NZ) % NZ, (y + dy) % 4, (c + dc) % 2)

    def member(dx=0, dc=0):
        return ((x + dx + NX) % NX) * 2 + (c + dc) % 2

    def send(src, dst, ss, rs, dev):
        copy = pltpu.make_async_remote_copy(src_ref=src, dst_ref=dst, send_sem=ss, recv_sem=rs,
                                            device_id=dev, device_id_type=MESH)
        copy.start()
        return copy

    sent = []
    peers = [at(dz=1), at(dz=-1), at(dx=1), at(dx=-1), at(dc=1), at(dy=1), at(dy=2), at(dy=3)]
    barrier = pltpu.get_barrier_semaphore()
    for dev in peers:
        pl.semaphore_signal(barrier, inc=1, device_id=dev, device_id_type=MESH)
    pl.semaphore_wait(barrier, len(peers))

    def part(ref, h):
        return ref.at[pl.ds(h * half, half)]

    tok = {}

    def tok_send(d, k, o):
        h = o if d == 0 else 1 - o
        src = tokens if k == 0 else tokbuf.at[2 * k - 2 + d]
        dst = last if k == 3 else tokbuf.at[2 * k + d]
        tok[d, k, o] = send(part(src, h), part(dst, h), tok_s.at[d, k, o], tok_r.at[d, k, o],
                            at(dz=1 if d == 0 else -1))
        sent.append(tok[d, k, o])

    tg = {}

    def tgt_send(d, k):
        src = 0 if k == 0 else 2 * k - 1 + d
        dst = 7 if k == 3 else 2 * k + 1 + d
        tg[d, k] = send(tgt.at[src], tgt.at[dst], tgt_s.at[d, k], tgt_r.at[d, k], at(dz=1 if d == 0 else -1))
        sent.append(tg[d, k])

    wc = {}
    store = (enc_all, dec_all, dec_all, bias_all)
    own = (enc, dec, dec, bias)
    side = width // 2

    def w_send(kind, slot, m, dev, first=False, piece=None):
        dst = store[kind].at[m]
        src = own[kind] if first else dst
        n = src.shape[0] if piece is None else src.shape[0] // 2
        rs_ = pl.ds(0 if piece is None else piece * n, n)
        if kind in (1, 2):
            cs = pl.ds((kind - 1) * side, side)
            src, dst = src.at[rs_, cs], dst.at[rs_, cs]
        elif kind == 0:
            src, dst = src.at[rs_], dst.at[rs_]
        wc[kind, slot] = send(src, dst, w_s.at[kind, slot], w_r.at[kind, slot], dev)
        sent.append(wc[kind, slot])

    def w_first(kind):
        for p in range(2):
            w_send(kind, p, member(), at(dx=1), first=True, piece=p)
            w_send(kind, 3 - p, member(), at(dx=-1), first=True, piece=1 - p)
        w_send(kind, 6, member(), at(dc=1), first=True)

    def w_pass(kind):
        wc[kind, 0].wait_recv()
        w_send(kind, 4, member(-1), at(dx=1), piece=0)
        wc[kind, 3].wait_recv()
        w_send(kind, 5, member(1), at(dx=-1), piece=1)

    def w_mid(kind):
        wc[kind, 1].wait_recv()
        w_send(kind, 7, member(-1), at(dc=1))
        wc[kind, 2].wait_recv()
        w_send(kind, 8, member(1), at(dc=1))

    def w_last(kind):
        for p in range(2):
            wc[kind, 4 + p].wait_recv()
            w_send(kind, 9 + p, member(2), at(dc=1), piece=p)

    def w_done(kind, slots):
        for slot in slots:
            wc[kind, slot].wait_recv()

    def b_first():
        w_send(3, 0, member(), at(dx=1), first=True)
        w_send(3, 1, member(), at(dx=-1), first=True)
        w_send(3, 6, member(), at(dc=1), first=True)

    def b_pass():
        wc[3, 0].wait_recv()
        w_send(3, 4, member(-1), at(dx=1))
        w_send(3, 7, member(-1), at(dc=1))
        wc[3, 1].wait_recv()
        w_send(3, 8, member(1), at(dc=1))

    def b_last():
        wc[3, 4].wait_recv()
        w_send(3, 9, member(2), at(dc=1))

    tok_send(0, 0, 0)
    tok_send(1, 0, 0)
    tok_send(0, 0, 1)
    tok_send(1, 0, 1)
    b_first()
    w_first(0)
    local = [pltpu.make_async_copy(tokens, stage, loc.at[0]),
             pltpu.make_async_copy(enc, enc_all.at[member()], loc.at[1]),
             pltpu.make_async_copy(dec, dec_all.at[member()], loc.at[2]),
             pltpu.make_async_copy(bias, bias_all.at[member()], loc.at[3])]
    for copy in local:
        copy.start()

    ids = lax.broadcasted_iota(jnp.int32, (blocks, rows), 0)
    hits = [act[pl.ds(k, 1), :] == ids for k in range(4)]
    named = (hits[0] | hits[1]) | (hits[2] | hits[3])
    before = (lax.broadcasted_iota(jnp.int32, (rows, rows), 0)
              < lax.broadcasted_iota(jnp.int32, (rows, rows), 1))
    rank = jnp.dot(jnp.where(named, 1.0, 0.0).astype(BF), jnp.where(before, 1.0, 0.0).astype(BF),
                   preferred_element_type=F32)
    where_to = rank + table[...]
    for k in range(4):
        tgt[0, pl.ds(k, 1), :] = jnp.sum(jnp.where(hits[k], where_to, 0.0), axis=0, keepdims=True)
    tgt[0, pl.ds(4, 4), :] = jnp.full((4, rows), -1.0, F32)
    tgt_send(0, 0)
    tgt_send(1, 0)

    base = (z * slots).astype(F32)

    def encode(ref, i):
        def pick(j, carry):
            n = slots // 4
            r0 = pl.multiple_of(j * n, n)
            place = (lax.broadcasted_iota(jnp.int32, (n, rows), 0) + r0).astype(F32) + base
            t = tgt[i]
            hit = ((t[0:1] == place) | (t[1:2] == place)) | ((t[2:3] == place) | (t[3:4] == place))
            picks[pl.ds(r0, n), :] = jnp.where(hit, 1.0, 0.0).astype(BF)
            return carry

        lax.fori_loop(0, 4, pick, 0)

        def gather(j, carry):
            n = width // 4
            c0 = pl.multiple_of(j * n, n)
            got = jnp.dot(picks[...], ref[:, pl.ds(c0, n)], preferred_element_type=F32)
            work[0, :, pl.ds(c0, n)] = (got - dbias[:, pl.ds(c0, n)]).astype(BF)
            return carry

        lax.fori_loop(0, 4, gather, 0)

        def one(m, carry):
            for b in range(4):
                r0 = pl.multiple_of((m * 4 + b) * PAD, PAD)
                preact[i, pl.ds(r0, PAD), :] = jnp.dot(
                    work[0, pl.ds(r0, PAD), :], enc_all[m, :, pl.ds(b * 128, 128)], preferred_element_type=F32)
            return carry

        lax.fori_loop(0, 8, one, 0)

    ysum, ycode = {}, {}

    def y_start(g, i, n):
        for o in range(1, 4):
            to = pl.multiple_of(((y + o) % 4) * quarter, quarter)
            ysum[g, o] = send(preact.at[pl.ds(i, n), pl.ds(to, quarter)], parts_in.at[o - 1, pl.ds(i, n)],
                              ys_s.at[g, o - 1], ys_r.at[g, o - 1], at(dy=o))
            sent.append(ysum[g, o])

    mine = pl.multiple_of(y * quarter, quarter)

    def y_codes(g, i, n):
        for o in range(1, 4):
            ysum[g, o].wait_recv()
        per = bias_all[pl.ds(2 * y, 2)].reshape(quarter // PAD, 1, 128)
        for j in range(i, i + n):
            total = preact[j, pl.ds(mine, quarter), :] + parts_in[0, j] + parts_in[1, j] + parts_in[2, j]
            total = total.reshape(quarter // PAD, PAD, 128) + per
            codes[j, pl.ds(mine, quarter), :] = jnp.maximum(total, 0.0).astype(BF).reshape(quarter, 128)
        for o in range(1, 4):
            view = codes.at[pl.ds(i, n), pl.ds(mine, quarter)]
            ycode[g, o] = send(view, view, yc_s.at[g, o - 1], yc_r.at[g, o - 1], at(dy=o))
            sent.append(ycode[g, o])

    def y_done(g):
        for o in range(1, 4):
            ycode[g, o].wait_recv()

    def tok_pass(k, o):
        for d in range(2):
            tok[d, k, o].wait_recv()
            if k < 2 or o == 0:
                tok_send(d, k + 1, o)

    def tgt_pass(k):
        for d in range(2):
            tg[d, k].wait_recv()
            if k < 2 or d == 0:
                tgt_send(d, k + 1)

    def staged(g):
        def step(j, carry):
            i = 2 * g - 1 + j
            copy = pltpu.make_async_copy(tokbuf.at[i - 1], stage, loc.at[4])
            copy.start()
            copy.wait()
            encode(stage, i)
            return carry

        lax.fori_loop(0, 2, step, 0)
        y_start(g, 2 * g - 1, 2)

    def decode(i, buf, q):
        cs = pl.ds(q * side, side)

        def one(m, carry):
            for b in range(4):
                r0 = pl.multiple_of((m * 4 + b) * PAD, PAD)
                work[buf, pl.ds(r0, PAD), cs] = jnp.dot(
                    codes[i, pl.ds(r0, PAD), :], dec_all[m, pl.ds(b * 128, 128), cs],
                    preferred_element_type=F32).astype(BF)
            return carry

        lax.fori_loop(0, 8, one, 0)

    def spread(i, h):
        t = jnp.concatenate([tgt[i], jnp.zeros((120, rows), F32)], axis=0)
        cols = jnp.transpose(t)[h * half:(h + 1) * half]
        place = lax.broadcasted_iota(jnp.int32, (half, slots), 1).astype(F32) + base
        hit = (((cols[:, 0:1] == place) | (cols[:, 1:2] == place))
               | ((cols[:, 2:3] == place) | (cols[:, 3:4] == place)))
        return jnp.where(hit, 1.0, 0.0).astype(BF)

    def tiles(q):
        n = side // 2
        return [pl.ds(q * side + j * n, n) for j in range(2)]

    def sums(h, buf, q, plus):
        for cs in tiles(q):
            total = jnp.dot(sels[h], work[buf, :, cs], preferred_element_type=F32)
            for ref in plus:
                total = total + ref[:, cs].astype(F32)
            yield cs, total

    def combine(h, buf, q, dst, plus=()):
        for cs, total in sums(h, buf, q, plus):
            dst[:, cs] = total.astype(BF)

    rs = {}

    def rs_send(d, q, k, o, src):
        cs = pl.ds(q * side, side)
        rs[d, q, k, o] = send(src.at[:, cs], rs_in.at[d, k, o, :, cs], rs_s.at[d, q, k, o], rs_r.at[d, q, k, o],
                              at(dz=1 if d == 0 else -1))
        if k > 1 or (k == 1 and o == 0):
            sent.append(rs[d, q, k, o])

    def ring_start(q):
        decode(7, 0, q)
        for d in range(2):
            sels[d] = spread(7, d)
            combine(d, 0, q, rs_first.at[d, 0])
            rs_send(d, q, 0, 0, rs_first.at[d, 0])
        for d in range(2):
            decode(5 + (1 - d), d, q)
            sels[1 - d] = spread(5 + (1 - d), 1 - d)
            combine(1 - d, d, q, rs_first.at[d, 1])
            rs_send(d, q, 1, 1, rs_first.at[d, 1])

    def ring_step(q, k):
        idx = (8 - 2 * k, 7 - 2 * k)
        for d in range(2):
            if k > 1:
                decode(idx[d], d, q)
        for o in range(1 if k == 1 else 2):
            for d in range(2):
                got = rs_in.at[d, k - 1, o]
                h = o if d == 0 else 1 - o
                sels[h] = spread(idx[d], h)
                rs[d, q, k - 1, o].wait_recv()
                combine(h, d, q, got, (got,))
                rs_send(d, q, k, o, got)

    def ring_end(q):
        decode(0, 0, q)
        for d in range(2):
            rs[d, q, 0, 0].wait_send()
            rs[d, q, 1, 1].wait_send()
            sels[d] = spread(0, d)
        for d in range(2):
            rs[d, q, 3, 0].wait_recv()
            for cs, total in sums(d, 0, q, (rs_in.at[d, 3, 0], dbias)):
                top = total.astype(BF)
                rs_first[0, d, :, cs] = top
                rs_first[1, d, :, cs] = (total - top.astype(F32)).astype(BF)
        for d in range(2):
            h = 1 - d
            rs[d, q, 3, 1].wait_recv()
            for cs in tiles(q):
                total = rs_first[0, h, :, cs].astype(F32) + rs_first[1, h, :, cs].astype(F32)
                out[pl.ds(h * half, half), cs] = (total + rs_in[d, 3, 1, :, cs].astype(F32)).astype(BF)

    b_pass()
    tok_pass(0, 0)
    w_pass(0)
    w_first(1)
    tok_pass(0, 1)
    tgt_pass(0)
    w_mid(0)
    b_last()
    tok_pass(1, 0)
    for copy in local:
        copy.wait()
    tok_pass(1, 1)
    tgt_pass(1)
    w_last(0)
    w_done(3, (6, 7, 8, 9))
    w_done(0, (6, 7, 8, 9, 10))
    encode(stage, 0)
    y_start(0, 0, 1)
    w_pass(1)
    w_first(2)
    tok_pass(2, 0)
    staged(1)
    y_codes(0, 0, 1)
    w_mid(1)
    staged(2)
    tok_pass(2, 1)
    tgt_pass(2)
    y_codes(1, 1, 2)
    w_last(1)
    staged(3)
    y_codes(2, 3, 2)
    w_pass(2)
    tok[0, 3, 0].wait_recv()
    tok[1, 3, 0].wait_recv()
    tg[0, 3].wait_recv()
    encode(last, 7)
    y_start(4, 7, 1)
    y_codes(3, 5, 2)
    w_mid(2)
    y_codes(4, 7, 1)
    for g in range(5):
        y_done(g)
    w_done(1, (6, 7, 8, 9, 10))
    ring_start(0)
    ring_step(0, 1)
    w_last(2)
    w_done(2, (6, 7, 8, 9, 10))
    ring_step(0, 2)
    ring_start(1)
    ring_step(0, 3)
    ring_step(1, 1)
    ring_end(0)
    ring_step(1, 2)
    ring_step(1, 3)
    ring_end(1)
    for copy in sent:
        copy.wait_send()


def local(tokens, active, placement_map, enc_weight, enc_bias, dec_weight, dec_bias):
    rows, width = tokens.shape
    blocks = placement_map.shape[0]
    slots = blocks // NZ * PAD
    depth = enc_weight.shape[1]
    p = placement_map
    table = ((p // 8) % NZ * slots + (p // (8 * NZ) * 8 + p % 8) * PAD).astype(F32).reshape(blocks, 1)
    vmem, hbm = pl.BlockSpec(memory_space=pltpu.VMEM), pl.BlockSpec(memory_space=pl.ANY)
    half = rows // 2
    dma = pltpu.SemaphoreType.DMA
    out, _ = pl.pallas_call(
        kernel,
        out_shape=(jax.ShapeDtypeStruct((rows, width), BF), jax.ShapeDtypeStruct((6, rows, width), BF)),
        in_specs=[hbm, vmem, vmem, hbm, vmem, hbm, vmem],
        out_specs=(vmem, hbm),
        scratch_shapes=[
            pltpu.VMEM((8, width, depth), BF),
            pltpu.VMEM((8, depth, width), BF),
            pltpu.VMEM((8, 4, 128), F32),
            pltpu.VMEM((8, 8, rows), F32),
            pltpu.VMEM((rows, width), BF),
            pltpu.VMEM((rows, width), BF),
            pltpu.VMEM((2, slots, width), BF),
            pltpu.VMEM((slots, rows), BF),
            pltpu.VMEM((8, slots, 128), F32),
            pltpu.VMEM((3, 8, slots // 4, 128), F32),
            pltpu.VMEM((8, slots, 128), BF),
            pltpu.VMEM((2, half, slots), BF),
            pltpu.VMEM((2, 2, half, width), BF),
            pltpu.VMEM((2, 4, 2, half, width), BF),
            dma((2, 4, 2)), dma((2, 4, 2)),
            dma((2, 4)), dma((2, 4)),
            dma((4, 11)), dma((4, 11)),
            dma((5, 3)), dma((5, 3)),
            dma((5, 3)), dma((5, 3)),
            dma((2, 2, 4, 2)), dma((2, 2, 4, 2)),
            dma((5,)),
        ],
        compiler_params=pltpu.CompilerParams(collective_id=0, has_side_effects=True, vmem_limit_bytes=63 << 20),
        name="encode_decode",
    )(tokens, active.T, table, enc_weight, enc_bias.reshape(4, 128), dec_weight, dec_bias.reshape(1, width))
    return out


def solution(mesh):
    return jax.shard_map(
        local,
        mesh=mesh,
        in_specs=(
            P(("seq", "lat"), "tp"),
            P(("seq", "lat"), None),
            P(),
            P("tp", ("seq", "lat")),
            P(("seq", "lat")),
            P(("seq", "lat"), "tp"),
            P("tp"),
        ),
        out_specs=P(("seq", "lat"), "tp"),
        check_vma=False,
    )
```

```python
import jax
import jax.numpy as jnp
from jax import lax
from jax.experimental import pallas as pl
from jax.experimental.pallas import tpu as pltpu
from jax.sharding import PartitionSpec as P

NX, NZ = 4, 8
PAD = 16
MESH = pl.DeviceIdType.MESH
BF, F32 = jnp.bfloat16, jnp.float32


def kernel(tokens, act, table, enc, bias, dec, dbias, out, tokbuf,
           enc_all, dec_all, bias_all, tgt, stage, last, work, picks, preact, parts_in, codes, sels,
           rs_first, rs_in,
           tok_s, tok_r, tgt_s, tgt_r, w_s, w_r, ys_s, ys_r, yc_s, yc_r, rs_s, rs_r, loc):
    rows, width = tokens.shape
    half = rows // 2
    blocks = table.shape[0]
    row_blocks = blocks // NZ
    slots = row_blocks * PAD
    quarter = slots // 4
    s, y, c = lax.axis_index("seq"), lax.axis_index("tp"), lax.axis_index("lat")
    x, z = s // NZ, s % NZ

    def at(dx=0, dz=0, dy=0, dc=0):
        return (((x + dx + NX) % NX) * NZ + (z + dz + NZ) % NZ, (y + dy) % 4, (c + dc) % 2)

    def member(dx=0, dc=0):
        return ((x + dx + NX) % NX) * 2 + (c + dc) % 2

    def send(src, dst, ss, rs, dev):
        copy = pltpu.make_async_remote_copy(src_ref=src, dst_ref=dst, send_sem=ss, recv_sem=rs,
                                            device_id=dev, device_id_type=MESH)
        copy.start()
        return copy

    sent = []
    peers = [at(dz=1), at(dz=-1), at(dx=1), at(dx=-1), at(dc=1), at(dy=1), at(dy=2), at(dy=3)]
    barrier = pltpu.get_barrier_semaphore()
    for dev in peers:
        pl.semaphore_signal(barrier, inc=1, device_id=dev, device_id_type=MESH)
    pl.semaphore_wait(barrier, len(peers))

    def part(ref, h):
        return ref.at[pl.ds(h * half, half)]

    tok = {}

    def tok_send(d, k, o):
        h = o if d == 0 else 1 - o
        src = tokens if k == 0 else tokbuf.at[2 * k - 2 + d]
        dst = last if k == 3 else tokbuf.at[2 * k + d]
        tok[d, k, o] = send(part(src, h), part(dst, h), tok_s.at[d, k, o], tok_r.at[d, k, o],
                            at(dz=1 if d == 0 else -1))
        sent.append(tok[d, k, o])

    tg = {}

    def tgt_send(d, k):
        src = 0 if k == 0 else 2 * k - 1 + d
        dst = 7 if k == 3 else 2 * k + 1 + d
        tg[d, k] = send(tgt.at[src], tgt.at[dst], tgt_s.at[d, k], tgt_r.at[d, k], at(dz=1 if d == 0 else -1))
        sent.append(tg[d, k])

    wc = {}
    store = (enc_all, dec_all, dec_all, bias_all)
    own = (enc, dec, dec, bias)
    side = width // 2

    def w_send(kind, slot, m, dev, first=False, piece=None):
        dst = store[kind].at[m]
        src = own[kind] if first else dst
        n = src.shape[0] if piece is None else src.shape[0] // 2
        rs_ = pl.ds(0 if piece is None else piece * n, n)
        if kind in (1, 2):
            cs = pl.ds((kind - 1) * side, side)
            src, dst = src.at[rs_, cs], dst.at[rs_, cs]
        elif kind == 0:
            src, dst = src.at[rs_], dst.at[rs_]
        wc[kind, slot] = send(src, dst, w_s.at[kind, slot], w_r.at[kind, slot], dev)
        sent.append(wc[kind, slot])

    def w_first(kind):
        for p in range(2):
            w_send(kind, p, member(), at(dx=1), first=True, piece=p)
            w_send(kind, 3 - p, member(), at(dx=-1), first=True, piece=1 - p)
        w_send(kind, 6, member(), at(dc=1), first=True)

    def w_pass(kind):
        wc[kind, 0].wait_recv()
        w_send(kind, 4, member(-1), at(dx=1), piece=0)
        wc[kind, 3].wait_recv()
        w_send(kind, 5, member(1), at(dx=-1), piece=1)

    def w_mid(kind):
        wc[kind, 1].wait_recv()
        w_send(kind, 7, member(-1), at(dc=1))
        wc[kind, 2].wait_recv()
        w_send(kind, 8, member(1), at(dc=1))

    def w_last(kind):
        for p in range(2):
            wc[kind, 4 + p].wait_recv()
            w_send(kind, 9 + p, member(2), at(dc=1), piece=p)

    def w_done(kind, slots):
        for slot in slots:
            wc[kind, slot].wait_recv()

    def b_first():
        w_send(3, 0, member(), at(dx=1), first=True)
        w_send(3, 1, member(), at(dx=-1), first=True)
        w_send(3, 6, member(), at(dc=1), first=True)

    def b_pass():
        wc[3, 0].wait_recv()
        w_send(3, 4, member(-1), at(dx=1))
        w_send(3, 7, member(-1), at(dc=1))
        wc[3, 1].wait_recv()
        w_send(3, 8, member(1), at(dc=1))

    def b_last():
        wc[3, 4].wait_recv()
        w_send(3, 9, member(2), at(dc=1))

    tok_send(0, 0, 0)
    tok_send(1, 0, 0)
    tok_send(0, 0, 1)
    tok_send(1, 0, 1)
    b_first()
    w_first(0)
    local = [pltpu.make_async_copy(tokens, stage, loc.at[0]),
             pltpu.make_async_copy(enc, enc_all.at[member()], loc.at[1]),
             pltpu.make_async_copy(dec, dec_all.at[member()], loc.at[2]),
             pltpu.make_async_copy(bias, bias_all.at[member()], loc.at[3])]
    for copy in local:
        copy.start()

    ids = lax.broadcasted_iota(jnp.int32, (blocks, rows), 0)
    hits = [act[pl.ds(k, 1), :] == ids for k in range(4)]
    named = (hits[0] | hits[1]) | (hits[2] | hits[3])
    before = (lax.broadcasted_iota(jnp.int32, (rows, rows), 0)
              < lax.broadcasted_iota(jnp.int32, (rows, rows), 1))
    rank = jnp.dot(jnp.where(named, 1.0, 0.0).astype(BF), jnp.where(before, 1.0, 0.0).astype(BF),
                   preferred_element_type=F32)
    where_to = rank + table[...]
    for k in range(4):
        tgt[0, pl.ds(k, 1), :] = jnp.sum(jnp.where(hits[k], where_to, 0.0), axis=0, keepdims=True)
    tgt[0, pl.ds(4, 4), :] = jnp.full((4, rows), -1.0, F32)
    tgt_send(0, 0)
    tgt_send(1, 0)

    base = (z * slots).astype(F32)

    def gather(ref, i, buf):
        def pick(j, carry):
            n = slots // 4
            r0 = pl.multiple_of(j * n, n)
            place = (lax.broadcasted_iota(jnp.int32, (n, rows), 0) + r0).astype(F32) + base
            t = tgt[i]
            hit = ((t[0:1] == place) | (t[1:2] == place)) | ((t[2:3] == place) | (t[3:4] == place))
            picks[pl.ds(r0, n), :] = jnp.where(hit, 1.0, 0.0).astype(BF)
            return carry

        lax.fori_loop(0, 4, pick, 0)
        for j in range(8):
            cs = pl.ds(j * (width // 8), width // 8)
            got = jnp.dot(picks[...], ref[:, cs], preferred_element_type=F32)
            work[buf, :, cs] = (got - dbias[:, cs]).astype(BF)

    def encode(i, n):
        def one(j, carry):
            for b in range(8):
                r0 = pl.multiple_of((j * 8 + b) * PAD, PAD)
                got = jnp.dot(work[0:n, pl.ds(r0, PAD), :].reshape(n * PAD, width),
                              enc_all[j * 2 + b // 4, :, pl.ds(b % 4 * 128, 128)], preferred_element_type=F32)
                for t in range(n):
                    preact[i + t, pl.ds(r0, PAD), :] = got[t * PAD:(t + 1) * PAD]
            return carry

        lax.fori_loop(0, 4, one, 0)

    def load(i, dst, k):
        copy = pltpu.make_async_copy(tokbuf.at[i - 1], dst, loc.at[k])
        copy.start()
        return copy

    ysum, ycode = {}, {}

    def y_start(g, i, n):
        for o in range(1, 4):
            to = pl.multiple_of(((y + o) % 4) * quarter, quarter)
            ysum[g, o] = send(preact.at[pl.ds(i, n), pl.ds(to, quarter)], parts_in.at[o - 1, pl.ds(i, n)],
                              ys_s.at[g, o - 1], ys_r.at[g, o - 1], at(dy=o))
            sent.append(ysum[g, o])

    mine = pl.multiple_of(y * quarter, quarter)

    def y_codes(g, i, n):
        for o in range(1, 4):
            ysum[g, o].wait_recv()
        per = bias_all[pl.ds(2 * y, 2)].reshape(quarter // PAD, 1, 128)
        for j in range(i, i + n):
            total = preact[j, pl.ds(mine, quarter), :] + parts_in[0, j] + parts_in[1, j] + parts_in[2, j]
            total = total.reshape(quarter // PAD, PAD, 128) + per
            codes[j, pl.ds(mine, quarter), :] = jnp.maximum(total, 0.0).astype(BF).reshape(quarter, 128)
        for o in range(1, 4):
            view = codes.at[pl.ds(i, n), pl.ds(mine, quarter)]
            ycode[g, o] = send(view, view, yc_s.at[g, o - 1], yc_r.at[g, o - 1], at(dy=o))
            sent.append(ycode[g, o])

    def y_done(g):
        for o in range(1, 4):
            ycode[g, o].wait_recv()

    def tok_pass(k, o):
        for d in range(2):
            tok[d, k, o].wait_recv()
            if k < 2 or o == 0:
                tok_send(d, k + 1, o)

    def tgt_pass(k):
        for d in range(2):
            tg[d, k].wait_recv()
            if k < 2 or d == 0:
                tgt_send(d, k + 1)

    def decode(i, buf, q):
        cs = pl.ds(q * side, side)

        def one(m, carry):
            for b in range(4):
                r0 = pl.multiple_of((m * 4 + b) * PAD, PAD)
                work[buf, pl.ds(r0, PAD), cs] = jnp.dot(
                    codes[i, pl.ds(r0, PAD), :], dec_all[m, pl.ds(b * 128, 128), cs],
                    preferred_element_type=F32).astype(BF)
            return carry

        lax.fori_loop(0, 8, one, 0)

    def spread(i, h):
        t = jnp.concatenate([tgt[i], jnp.zeros((120, rows), F32)], axis=0)
        cols = jnp.transpose(t)[h * half:(h + 1) * half]
        place = lax.broadcasted_iota(jnp.int32, (half, slots), 1).astype(F32) + base
        hit = (((cols[:, 0:1] == place) | (cols[:, 1:2] == place))
               | ((cols[:, 2:3] == place) | (cols[:, 3:4] == place)))
        return jnp.where(hit, 1.0, 0.0).astype(BF)

    def tiles(q):
        n = side // 2
        return [pl.ds(q * side + j * n, n) for j in range(2)]

    def sums(h, buf, q, plus):
        for cs in tiles(q):
            total = jnp.dot(sels[h], work[buf, :, cs], preferred_element_type=F32)
            for ref in plus:
                total = total + ref[:, cs].astype(F32)
            yield cs, total

    def combine(h, buf, q, dst, plus=()):
        for cs, total in sums(h, buf, q, plus):
            dst[:, cs] = total.astype(BF)

    rs = {}

    def rs_send(d, q, k, o, src):
        cs = pl.ds(q * side, side)
        rs[d, q, k, o] = send(src.at[:, cs], rs_in.at[d, k, o, :, cs], rs_s.at[d, q, k, o], rs_r.at[d, q, k, o],
                              at(dz=1 if d == 0 else -1))
        if k > 1 or (k == 1 and o == 0):
            sent.append(rs[d, q, k, o])

    def ring_start(q):
        decode(7, 0, q)
        for d in range(2):
            sels[d] = spread(7, d)
            combine(d, 0, q, rs_first.at[d, 0])
            rs_send(d, q, 0, 0, rs_first.at[d, 0])
        for d in range(2):
            decode(5 + (1 - d), d, q)
            sels[1 - d] = spread(5 + (1 - d), 1 - d)
            combine(1 - d, d, q, rs_first.at[d, 1])
            rs_send(d, q, 1, 1, rs_first.at[d, 1])

    def ring_step(q, k):
        idx = (8 - 2 * k, 7 - 2 * k)
        for d in range(2):
            if k > 1:
                decode(idx[d], d, q)
        for o in range(1 if k == 1 else 2):
            for d in range(2):
                got = rs_in.at[d, k - 1, o]
                h = o if d == 0 else 1 - o
                sels[h] = spread(idx[d], h)
                rs[d, q, k - 1, o].wait_recv()
                combine(h, d, q, got, (got,))
                rs_send(d, q, k, o, got)

    def ring_end(q):
        decode(0, 0, q)
        for d in range(2):
            rs[d, q, 0, 0].wait_send()
            rs[d, q, 1, 1].wait_send()
            sels[d] = spread(0, d)
        for d in range(2):
            rs[d, q, 3, 0].wait_recv()
            for cs, total in sums(d, 0, q, (rs_in.at[d, 3, 0], dbias)):
                top = total.astype(BF)
                rs_first[0, d, :, cs] = top
                rs_first[1, d, :, cs] = (total - top.astype(F32)).astype(BF)
        for d in range(2):
            h = 1 - d
            rs[d, q, 3, 1].wait_recv()
            for cs in tiles(q):
                total = rs_first[0, h, :, cs].astype(F32) + rs_first[1, h, :, cs].astype(F32)
                out[pl.ds(h * half, half), cs] = (total + rs_in[d, 3, 1, :, cs].astype(F32)).astype(BF)

    b_pass()
    tok_pass(0, 0)
    w_pass(0)
    w_first(1)
    tok_pass(0, 1)
    tgt_pass(0)
    one = load(1, out, 5)
    for copy in local:
        copy.wait()
    gather(stage, 0, 0)
    two = load(2, stage, 4)
    one.wait()
    gather(out, 1, 1)
    w_mid(0)
    b_last()
    tok_pass(1, 0)
    tok_pass(1, 1)
    tgt_pass(1)
    three = load(3, out, 5)
    w_last(0)
    w_done(3, (6, 7, 8, 9))
    w_done(0, (6, 7, 8, 9, 10))
    encode(0, 2)
    y_start(0, 0, 2)
    w_pass(1)
    w_first(2)
    two.wait()
    gather(stage, 2, 0)
    four = load(4, stage, 4)
    three.wait()
    gather(out, 3, 1)
    encode(2, 2)
    tok_pass(2, 0)
    four.wait()
    gather(stage, 4, 0)
    encode(4, 1)
    y_start(1, 2, 3)
    y_codes(0, 0, 2)
    w_mid(1)
    tok_pass(2, 1)
    tgt_pass(2)
    five, six = load(5, stage, 4), load(6, out, 5)
    w_last(1)
    five.wait()
    gather(stage, 5, 0)
    six.wait()
    gather(out, 6, 1)
    encode(5, 2)
    y_start(2, 5, 2)
    y_codes(1, 2, 3)
    w_pass(2)
    tg[0, 3].wait_recv()
    tok[0, 3, 0].wait_recv()
    tok[1, 3, 0].wait_recv()
    gather(last, 7, 0)
    encode(7, 1)
    y_start(3, 7, 1)
    y_codes(2, 5, 2)
    for g in range(3):
        y_done(g)
    w_done(1, (6, 7, 8, 9, 10))
    y_codes(3, 7, 1)
    w_mid(2)
    y_done(3)
    ring_start(0)
    ring_step(0, 1)
    w_last(2)
    ring_step(0, 2)
    w_done(2, (6, 7, 8, 9, 10))
    ring_start(1)
    ring_step(0, 3)
    ring_step(1, 1)
    ring_end(0)
    ring_step(1, 2)
    ring_step(1, 3)
    ring_end(1)
    for copy in sent:
        copy.wait_send()


def local(tokens, active, placement_map, enc_weight, enc_bias, dec_weight, dec_bias):
    rows, width = tokens.shape
    blocks = placement_map.shape[0]
    slots = blocks // NZ * PAD
    depth = enc_weight.shape[1]
    p = placement_map
    table = ((p // 8) % NZ * slots + (p // (8 * NZ) * 8 + p % 8) * PAD).astype(F32).reshape(blocks, 1)
    vmem, hbm = pl.BlockSpec(memory_space=pltpu.VMEM), pl.BlockSpec(memory_space=pl.ANY)
    half = rows // 2
    dma = pltpu.SemaphoreType.DMA
    out, _ = pl.pallas_call(
        kernel,
        out_shape=(jax.ShapeDtypeStruct((rows, width), BF), jax.ShapeDtypeStruct((6, rows, width), BF)),
        in_specs=[hbm, vmem, vmem, hbm, vmem, hbm, vmem],
        out_specs=(vmem, hbm),
        scratch_shapes=[
            pltpu.VMEM((8, width, depth), BF),
            pltpu.VMEM((8, depth, width), BF),
            pltpu.VMEM((8, 4, 128), F32),
            pltpu.VMEM((8, 8, rows), F32),
            pltpu.VMEM((rows, width), BF),
            pltpu.VMEM((rows, width), BF),
            pltpu.VMEM((2, slots, width), BF),
            pltpu.VMEM((slots, rows), BF),
            pltpu.VMEM((8, slots, 128), F32),
            pltpu.VMEM((3, 8, slots // 4, 128), F32),
            pltpu.VMEM((8, slots, 128), BF),
            pltpu.VMEM((2, half, slots), BF),
            pltpu.VMEM((2, 2, half, width), BF),
            pltpu.VMEM((2, 4, 2, half, width), BF),
            dma((2, 4, 2)), dma((2, 4, 2)),
            dma((2, 4)), dma((2, 4)),
            dma((4, 11)), dma((4, 11)),
            dma((4, 3)), dma((4, 3)),
            dma((4, 3)), dma((4, 3)),
            dma((2, 2, 4, 2)), dma((2, 2, 4, 2)),
            dma((6,)),
        ],
        compiler_params=pltpu.CompilerParams(collective_id=0, has_side_effects=True, vmem_limit_bytes=63 << 20),
        name="encode_decode",
    )(tokens, active.T, table, enc_weight, enc_bias.reshape(4, 128), dec_weight, dec_bias.reshape(1, width))
    return out


def solution(mesh):
    return jax.shard_map(
        local,
        mesh=mesh,
        in_specs=(
            P(("seq", "lat"), "tp"),
            P(("seq", "lat"), None),
            P(),
            P("tp", ("seq", "lat")),
            P(("seq", "lat")),
            P(("seq", "lat"), "tp"),
            P("tp"),
        ),
        out_specs=P(("seq", "lat"), "tp"),
        check_vma=False,
    )
```

```python
import jax
import jax.numpy as jnp
from jax import lax
from jax.experimental import pallas as pl
from jax.experimental.pallas import tpu as pltpu
from jax.sharding import PartitionSpec as P

NX, NZ = 4, 8
PAD = 16
MESH = pl.DeviceIdType.MESH
BF, F32 = jnp.bfloat16, jnp.float32


def kernel(tokens, act, table, enc, bias, dec, dbias, out, tokbuf,
           enc_all, dec_all, bias_all, tgt, stage, last, work, picks, preact, parts_in, codes, sels,
           rs_first, rs_in,
           tok_s, tok_r, tgt_s, tgt_r, w_s, w_r, ys_s, ys_r, yc_s, yc_r, rs_s, rs_r, loc):
    rows, width = tokens.shape
    half = rows // 2
    blocks = table.shape[0]
    row_blocks = blocks // NZ
    slots = row_blocks * PAD
    quarter = slots // 4
    s, y, c = lax.axis_index("seq"), lax.axis_index("tp"), lax.axis_index("lat")
    x, z = s // NZ, s % NZ

    def at(dx=0, dz=0, dy=0, dc=0):
        return (((x + dx + NX) % NX) * NZ + (z + dz + NZ) % NZ, (y + dy) % 4, (c + dc) % 2)

    def member(dx=0, dc=0):
        return ((x + dx + NX) % NX) * 2 + (c + dc) % 2

    def send(src, dst, ss, rs, dev):
        copy = pltpu.make_async_remote_copy(src_ref=src, dst_ref=dst, send_sem=ss, recv_sem=rs,
                                            device_id=dev, device_id_type=MESH)
        copy.start()
        return copy

    sent = []
    peers = [at(dz=1), at(dz=-1), at(dx=1), at(dx=-1), at(dc=1), at(dy=1), at(dy=2), at(dy=3)]
    barrier = pltpu.get_barrier_semaphore()
    for dev in peers:
        pl.semaphore_signal(barrier, inc=1, device_id=dev, device_id_type=MESH)
    pl.semaphore_wait(barrier, len(peers))

    def part(ref, h):
        return ref.at[pl.ds(h * half, half)]

    tok = {}

    def tok_send(d, k, o):
        h = o if d == 0 else 1 - o
        src = tokens if k == 0 else tokbuf.at[2 * k - 2 + d]
        dst = last if k == 3 else tokbuf.at[2 * k + d]
        tok[d, k, o] = send(part(src, h), part(dst, h), tok_s.at[d, k, o], tok_r.at[d, k, o],
                            at(dz=1 if d == 0 else -1))
        sent.append(tok[d, k, o])

    tg = {}

    def tgt_send(d, k):
        src = 0 if k == 0 else 2 * k - 1 + d
        dst = 7 if k == 3 else 2 * k + 1 + d
        tg[d, k] = send(tgt.at[src], tgt.at[dst], tgt_s.at[d, k], tgt_r.at[d, k], at(dz=1 if d == 0 else -1))
        sent.append(tg[d, k])

    wc = {}
    store = (enc_all, dec_all, dec_all, bias_all)
    own = (enc, dec, dec, bias)
    side = width // 2

    def w_send(kind, slot, m, dev, first=False, piece=None):
        dst = store[kind].at[m]
        src = own[kind] if first else dst
        n = src.shape[0] if piece is None else src.shape[0] // 2
        rs_ = pl.ds(0 if piece is None else piece * n, n)
        if kind in (1, 2):
            cs = pl.ds((kind - 1) * side, side)
            src, dst = src.at[rs_, cs], dst.at[rs_, cs]
        elif kind == 0:
            src, dst = src.at[rs_], dst.at[rs_]
        wc[kind, slot] = send(src, dst, w_s.at[kind, slot], w_r.at[kind, slot], dev)
        sent.append(wc[kind, slot])

    def w_first(kind):
        for p in range(2):
            w_send(kind, p, member(), at(dx=1), first=True, piece=p)
            w_send(kind, 3 - p, member(), at(dx=-1), first=True, piece=1 - p)
        w_send(kind, 6, member(), at(dc=1), first=True)

    def w_pass(kind):
        wc[kind, 0].wait_recv()
        w_send(kind, 4, member(-1), at(dx=1), piece=0)
        wc[kind, 3].wait_recv()
        w_send(kind, 5, member(1), at(dx=-1), piece=1)

    def w_mid(kind):
        wc[kind, 1].wait_recv()
        w_send(kind, 7, member(-1), at(dc=1))
        wc[kind, 2].wait_recv()
        w_send(kind, 8, member(1), at(dc=1))

    def w_last(kind):
        for p in range(2):
            wc[kind, 4 + p].wait_recv()
            w_send(kind, 9 + p, member(2), at(dc=1), piece=p)

    def w_done(kind, slots):
        for slot in slots:
            wc[kind, slot].wait_recv()

    def b_first():
        w_send(3, 0, member(), at(dx=1), first=True)
        w_send(3, 1, member(), at(dx=-1), first=True)
        w_send(3, 6, member(), at(dc=1), first=True)

    def b_pass():
        wc[3, 0].wait_recv()
        w_send(3, 4, member(-1), at(dx=1))
        w_send(3, 7, member(-1), at(dc=1))
        wc[3, 1].wait_recv()
        w_send(3, 8, member(1), at(dc=1))

    def b_last():
        wc[3, 4].wait_recv()
        w_send(3, 9, member(2), at(dc=1))

    tok_send(0, 0, 0)
    tok_send(1, 0, 0)
    tok_send(0, 0, 1)
    tok_send(1, 0, 1)
    b_first()
    w_first(0)
    local = [pltpu.make_async_copy(tokens, stage, loc.at[0]),
             pltpu.make_async_copy(enc, enc_all.at[member()], loc.at[1]),
             pltpu.make_async_copy(dec, dec_all.at[member()], loc.at[2]),
             pltpu.make_async_copy(bias, bias_all.at[member()], loc.at[3])]
    for copy in local:
        copy.start()

    ids = lax.broadcasted_iota(jnp.int32, (blocks, rows), 0)
    hits = [act[pl.ds(k, 1), :] == ids for k in range(4)]
    named = (hits[0] | hits[1]) | (hits[2] | hits[3])
    before = (lax.broadcasted_iota(jnp.int32, (rows, rows), 0)
              < lax.broadcasted_iota(jnp.int32, (rows, rows), 1))
    rank = jnp.dot(jnp.where(named, 1.0, 0.0).astype(BF), jnp.where(before, 1.0, 0.0).astype(BF),
                   preferred_element_type=F32)
    where_to = rank + table[...]
    for k in range(4):
        tgt[0, pl.ds(k, 1), :] = jnp.sum(jnp.where(hits[k], where_to, 0.0), axis=0, keepdims=True)
    tgt[0, pl.ds(4, 4), :] = jnp.full((4, rows), -1.0, F32)
    tgt_send(0, 0)
    tgt_send(1, 0)

    base = (z * slots).astype(F32)

    def gather(ref, i, buf):
        def pick(j, carry):
            n = slots // 4
            r0 = pl.multiple_of(j * n, n)
            place = (lax.broadcasted_iota(jnp.int32, (n, rows), 0) + r0).astype(F32) + base
            t = tgt[i]
            hit = ((t[0:1] == place) | (t[1:2] == place)) | ((t[2:3] == place) | (t[3:4] == place))
            picks[pl.ds(r0, n), :] = jnp.where(hit, 1.0, 0.0).astype(BF)
            return carry

        lax.fori_loop(0, 4, pick, 0)
        def product(j, carry):
            for t in range(4):
                n = width // 8
                cs = pl.ds(pl.multiple_of((j * 4 + t) * n, n), n)
                got = jnp.dot(picks[...], ref[:, cs], preferred_element_type=F32)
                work[buf, :, cs] = (got - dbias[:, cs]).astype(BF)
            return carry

        lax.fori_loop(0, 2, product, 0)

    def encode(i, n):
        def one(j, carry):
            for b in range(8):
                r0 = pl.multiple_of((j * 8 + b) * PAD, PAD)
                got = jnp.dot(work[0:n, pl.ds(r0, PAD), :].reshape(n * PAD, width),
                              enc_all[j * 2 + b // 4, :, pl.ds(b % 4 * 128, 128)], preferred_element_type=F32)
                for t in range(n):
                    preact[i + t, pl.ds(r0, PAD), :] = got[t * PAD:(t + 1) * PAD]
            return carry

        lax.fori_loop(0, 4, one, 0)

    def load(i, dst, k):
        copy = pltpu.make_async_copy(tokbuf.at[i - 1], dst, loc.at[k])
        copy.start()
        return copy

    ysum, ycode = {}, {}

    def y_start(g, i, n):
        for o in range(1, 4):
            to = pl.multiple_of(((y + o) % 4) * quarter, quarter)
            ysum[g, o] = send(preact.at[pl.ds(i, n), pl.ds(to, quarter)], parts_in.at[o - 1, pl.ds(i, n)],
                              ys_s.at[g, o - 1], ys_r.at[g, o - 1], at(dy=o))
            sent.append(ysum[g, o])

    mine = pl.multiple_of(y * quarter, quarter)

    def y_codes(g, i, n):
        for o in range(1, 4):
            ysum[g, o].wait_recv()
        per = bias_all[pl.ds(2 * y, 2)].reshape(quarter // PAD, 1, 128)
        for j in range(i, i + n):
            total = preact[j, pl.ds(mine, quarter), :] + parts_in[0, j] + parts_in[1, j] + parts_in[2, j]
            total = total.reshape(quarter // PAD, PAD, 128) + per
            codes[j, pl.ds(mine, quarter), :] = jnp.maximum(total, 0.0).astype(BF).reshape(quarter, 128)
        for o in range(1, 4):
            view = codes.at[pl.ds(i, n), pl.ds(mine, quarter)]
            ycode[g, o] = send(view, view, yc_s.at[g, o - 1], yc_r.at[g, o - 1], at(dy=o))
            sent.append(ycode[g, o])

    def y_done(g):
        for o in range(1, 4):
            ycode[g, o].wait_recv()

    def tok_pass(k, o):
        for d in range(2):
            tok[d, k, o].wait_recv()
            if k < 2 or o == 0:
                tok_send(d, k + 1, o)

    def tgt_pass(k):
        for d in range(2):
            tg[d, k].wait_recv()
            if k < 2 or d == 0:
                tgt_send(d, k + 1)

    def decode(i, buf, q):
        cs = pl.ds(q * side, side)

        def one(m, carry):
            for b in range(4):
                r0 = pl.multiple_of((m * 4 + b) * PAD, PAD)
                work[buf, pl.ds(r0, PAD), cs] = jnp.dot(
                    codes[i, pl.ds(r0, PAD), :], dec_all[m, pl.ds(b * 128, 128), cs],
                    preferred_element_type=F32).astype(BF)
            return carry

        lax.fori_loop(0, 8, one, 0)

    def spread(i, h):
        t = jnp.concatenate([tgt[i], jnp.zeros((120, rows), F32)], axis=0)
        cols = jnp.transpose(t)[h * half:(h + 1) * half]
        place = lax.broadcasted_iota(jnp.int32, (half, slots), 1).astype(F32) + base
        hit = (((cols[:, 0:1] == place) | (cols[:, 1:2] == place))
               | ((cols[:, 2:3] == place) | (cols[:, 3:4] == place)))
        return jnp.where(hit, 1.0, 0.0).astype(BF)

    def tiles(q):
        n = side // 2
        return [pl.ds(q * side + j * n, n) for j in range(2)]

    def sums(h, buf, q, plus):
        for cs in tiles(q):
            total = jnp.dot(sels[h], work[buf, :, cs], preferred_element_type=F32)
            for ref in plus:
                total = total + ref[:, cs].astype(F32)
            yield cs, total

    def combine(h, buf, q, dst, plus=()):
        for cs, total in sums(h, buf, q, plus):
            dst[:, cs] = total.astype(BF)

    rs = {}

    def rs_send(d, q, k, o, src):
        cs = pl.ds(q * side, side)
        rs[d, q, k, o] = send(src.at[:, cs], rs_in.at[d, k, o, :, cs], rs_s.at[d, q, k, o], rs_r.at[d, q, k, o],
                              at(dz=1 if d == 0 else -1))
        if k > 1 or (k == 1 and o == 0):
            sent.append(rs[d, q, k, o])

    def decode_two(i, q):
        def one(d, carry):
            decode(i - d, d, q)
            return carry

        lax.fori_loop(0, 2, one, 0)

    def near_first(q):
        decode_two(6, q)
        for d in range(2):
            sels[1 - d] = spread(6 - d, 1 - d)
            combine(1 - d, d, q, rs_first.at[d, 1])
            rs_send(d, q, 1, 1, rs_first.at[d, 1])

    def far_first(q):
        decode(7, 0, q)
        for d in range(2):
            sels[d] = spread(7, d)
            combine(d, 0, q, rs_first.at[d, 0])
            rs_send(d, q, 0, 0, rs_first.at[d, 0])

    def ring_step(q, k, o):
        decode_two(8 - 2 * k, q)
        for d in range(2):
            got = rs_in.at[d, k - 1, o]
            h = o if d == 0 else 1 - o
            sels[h] = spread(8 - 2 * k - d, h)
            rs[d, q, k - 1, o].wait_recv()
            combine(h, d, q, got, (got,))
            rs_send(d, q, k, o, got)

    def ring_sum(q):
        decode(0, 0, q)
        for d in range(2):
            rs[d, q, 0, 0].wait_send()
            rs[d, q, 1, 1].wait_send()
            sels[d] = spread(0, d)
        for d in range(2):
            h = 1 - d
            rs[d, q, 3, 1].wait_recv()
            for cs, total in sums(h, 0, q, (rs_in.at[d, 3, 1], dbias)):
                top = total.astype(BF)
                rs_first[0, h, :, cs] = top
                rs_first[1, h, :, cs] = (total - top.astype(F32)).astype(BF)

    def ring_end(q):
        for d in range(2):
            rs[d, q, 3, 0].wait_recv()
            for cs in tiles(q):
                total = rs_first[0, d, :, cs].astype(F32) + rs_first[1, d, :, cs].astype(F32)
                out[pl.ds(d * half, half), cs] = (total + rs_in[d, 3, 0, :, cs].astype(F32)).astype(BF)

    b_pass()
    tok_pass(0, 0)
    w_pass(0)
    w_first(1)
    tok_pass(0, 1)
    tgt_pass(0)
    one = load(1, out, 5)
    for copy in local:
        copy.wait()
    gather(stage, 0, 0)
    two = load(2, stage, 4)
    one.wait()
    gather(out, 1, 1)
    w_mid(0)
    b_last()
    tok_pass(1, 0)
    tok_pass(1, 1)
    tgt_pass(1)
    three = load(3, out, 5)
    w_last(0)
    w_done(3, (6, 7, 8, 9))
    w_done(0, (6, 7, 8, 9, 10))
    encode(0, 2)
    y_start(0, 0, 2)
    w_pass(1)
    w_first(2)
    two.wait()
    gather(stage, 2, 0)
    four = load(4, stage, 4)
    three.wait()
    gather(out, 3, 1)
    encode(2, 2)
    tok_pass(2, 0)
    four.wait()
    gather(stage, 4, 0)
    encode(4, 1)
    y_start(1, 2, 3)
    y_codes(0, 0, 2)
    w_mid(1)
    tok_pass(2, 1)
    tgt_pass(2)
    five, six = load(5, stage, 4), load(6, out, 5)
    w_last(1)
    five.wait()
    gather(stage, 5, 0)
    six.wait()
    gather(out, 6, 1)
    encode(5, 2)
    y_start(2, 5, 2)
    y_codes(1, 2, 3)
    y_codes(2, 5, 2)
    w_done(1, (6, 7, 8, 9, 10))
    w_pass(2)
    for g in range(3):
        y_done(g)
    near_first(0)
    tg[0, 3].wait_recv()
    tok[0, 3, 0].wait_recv()
    tok[1, 3, 0].wait_recv()
    gather(last, 7, 0)
    encode(7, 1)
    y_start(3, 7, 1)
    w_mid(2)
    y_codes(3, 7, 1)
    ring_step(0, 2, 1)
    y_done(3)
    far_first(0)
    w_last(2)
    ring_step(0, 3, 1)
    w_done(2, (6, 7, 8, 9, 10))
    near_first(1)
    far_first(1)
    ring_step(0, 1, 0)
    ring_step(1, 2, 1)
    ring_step(1, 1, 0)
    ring_step(0, 2, 0)
    ring_step(1, 3, 1)
    ring_step(1, 2, 0)
    ring_sum(0)
    ring_step(0, 3, 0)
    ring_sum(1)
    ring_step(1, 3, 0)
    ring_end(0)
    ring_end(1)
    for copy in sent:
        copy.wait_send()


def local(tokens, active, placement_map, enc_weight, enc_bias, dec_weight, dec_bias):
    rows, width = tokens.shape
    blocks = placement_map.shape[0]
    slots = blocks // NZ * PAD
    depth = enc_weight.shape[1]
    p = placement_map
    table = ((p // 8) % NZ * slots + (p // (8 * NZ) * 8 + p % 8) * PAD).astype(F32).reshape(blocks, 1)
    vmem, hbm = pl.BlockSpec(memory_space=pltpu.VMEM), pl.BlockSpec(memory_space=pl.ANY)
    half = rows // 2
    dma = pltpu.SemaphoreType.DMA
    out, _ = pl.pallas_call(
        kernel,
        out_shape=(jax.ShapeDtypeStruct((rows, width), BF), jax.ShapeDtypeStruct((6, rows, width), BF)),
        in_specs=[hbm, vmem, vmem, hbm, vmem, hbm, vmem],
        out_specs=(vmem, hbm),
        scratch_shapes=[
            pltpu.VMEM((8, width, depth), BF),
            pltpu.VMEM((8, depth, width), BF),
            pltpu.VMEM((8, 4, 128), F32),
            pltpu.VMEM((8, 8, rows), F32),
            pltpu.VMEM((rows, width), BF),
            pltpu.VMEM((rows, width), BF),
            pltpu.VMEM((2, slots, width), BF),
            pltpu.VMEM((slots, rows), BF),
            pltpu.VMEM((8, slots, 128), F32),
            pltpu.VMEM((3, 8, slots // 4, 128), F32),
            pltpu.VMEM((8, slots, 128), BF),
            pltpu.VMEM((2, half, slots), BF),
            pltpu.VMEM((2, 2, half, width), BF),
            pltpu.VMEM((2, 4, 2, half, width), BF),
            dma((2, 4, 2)), dma((2, 4, 2)),
            dma((2, 4)), dma((2, 4)),
            dma((4, 11)), dma((4, 11)),
            dma((4, 3)), dma((4, 3)),
            dma((4, 3)), dma((4, 3)),
            dma((2, 2, 4, 2)), dma((2, 2, 4, 2)),
            dma((6,)),
        ],
        compiler_params=pltpu.CompilerParams(collective_id=0, has_side_effects=True, vmem_limit_bytes=63 << 20),
        name="encode_decode",
    )(tokens, active.T, table, enc_weight, enc_bias.reshape(4, 128), dec_weight, dec_bias.reshape(1, width))
    return out


def solution(mesh):
    return jax.shard_map(
        local,
        mesh=mesh,
        in_specs=(
            P(("seq", "lat"), "tp"),
            P(("seq", "lat"), None),
            P(),
            P("tp", ("seq", "lat")),
            P(("seq", "lat")),
            P(("seq", "lat"), "tp"),
            P("tp"),
        ),
        out_specs=P(("seq", "lat"), "tp"),
        check_vma=False,
    )
```

```python
import jax
import jax.numpy as jnp
from jax import lax
from jax.experimental import pallas as pl
from jax.experimental.pallas import tpu as pltpu
from jax.sharding import PartitionSpec as P

NX, NZ = 4, 8
PAD = 16
MESH = pl.DeviceIdType.MESH
BF, F32 = jnp.bfloat16, jnp.float32


def kernel(tokens, act, table, enc, bias, dec, dbias, out, tokbuf,
           enc_all, dec_all, bias_all, tgt, stage, last, work, picks, preact, parts_in, codes, sels,
           rs_first, rs_in,
           tok_s, tok_r, tgt_s, tgt_r, w_s, w_r, ys_s, ys_r, yc_s, yc_r, rs_s, rs_r, loc):
    rows, width = tokens.shape
    half = rows // 2
    blocks = table.shape[0]
    row_blocks = blocks // NZ
    slots = row_blocks * PAD
    quarter = slots // 4
    s, y, c = lax.axis_index("seq"), lax.axis_index("tp"), lax.axis_index("lat")
    x, z = s // NZ, s % NZ

    def at(dx=0, dz=0, dy=0, dc=0):
        return (((x + dx + NX) % NX) * NZ + (z + dz + NZ) % NZ, (y + dy) % 4, (c + dc) % 2)

    def member(dx=0, dc=0):
        return ((x + dx + NX) % NX) * 2 + (c + dc) % 2

    def send(src, dst, ss, rs, dev):
        copy = pltpu.make_async_remote_copy(src_ref=src, dst_ref=dst, send_sem=ss, recv_sem=rs,
                                            device_id=dev, device_id_type=MESH)
        copy.start()
        return copy

    sent = []
    peers = [at(dz=1), at(dz=-1), at(dx=1), at(dx=-1), at(dc=1), at(dy=1), at(dy=2), at(dy=3)]
    barrier = pltpu.get_barrier_semaphore()
    for dev in peers:
        pl.semaphore_signal(barrier, inc=1, device_id=dev, device_id_type=MESH)
    pl.semaphore_wait(barrier, len(peers))

    def part(ref, h):
        return ref.at[pl.ds(h * half, half)]

    tok = {}

    def tok_send(d, k, o):
        h = o if d == 0 else 1 - o
        src = tokens if k == 0 else tokbuf.at[2 * k - 2 + d]
        dst = last if k == 3 else tokbuf.at[2 * k + d]
        tok[d, k, o] = send(part(src, h), part(dst, h), tok_s.at[d, k, o], tok_r.at[d, k, o],
                            at(dz=1 if d == 0 else -1))
        sent.append(tok[d, k, o])

    tg = {}

    def tgt_send(d, k):
        src = 0 if k == 0 else 2 * k - 1 + d
        dst = 7 if k == 3 else 2 * k + 1 + d
        tg[d, k] = send(tgt.at[src], tgt.at[dst], tgt_s.at[d, k], tgt_r.at[d, k], at(dz=1 if d == 0 else -1))
        sent.append(tg[d, k])

    wc = {}
    store = (enc_all, dec_all, dec_all, bias_all)
    own = (enc, dec, dec, bias)
    side = width // 2

    def w_send(kind, slot, m, dev, first=False, piece=None):
        dst = store[kind].at[m]
        src = own[kind] if first else dst
        n = src.shape[0] if piece is None else src.shape[0] // 2
        rs_ = pl.ds(0 if piece is None else piece * n, n)
        if kind in (1, 2):
            cs = pl.ds((kind - 1) * side, side)
            src, dst = src.at[rs_, cs], dst.at[rs_, cs]
        elif kind == 0:
            src, dst = src.at[rs_], dst.at[rs_]
        wc[kind, slot] = send(src, dst, w_s.at[kind, slot], w_r.at[kind, slot], dev)
        sent.append(wc[kind, slot])

    def w_first(kind):
        for p in range(2):
            w_send(kind, p, member(), at(dx=1), first=True, piece=p)
            w_send(kind, 3 - p, member(), at(dx=-1), first=True, piece=1 - p)
        w_send(kind, 6, member(), at(dc=1), first=True)

    def w_pass(kind):
        wc[kind, 0].wait_recv()
        w_send(kind, 4, member(-1), at(dx=1), piece=0)
        wc[kind, 3].wait_recv()
        w_send(kind, 5, member(1), at(dx=-1), piece=1)

    def w_mid(kind):
        wc[kind, 1].wait_recv()
        w_send(kind, 7, member(-1), at(dc=1))
        wc[kind, 2].wait_recv()
        w_send(kind, 8, member(1), at(dc=1))

    def w_last(kind):
        for p in range(2):
            wc[kind, 4 + p].wait_recv()
            w_send(kind, 9 + p, member(2), at(dc=1), piece=p)

    def w_done(kind, slots):
        for slot in slots:
            wc[kind, slot].wait_recv()

    def b_first():
        w_send(3, 0, member(), at(dx=1), first=True)
        w_send(3, 1, member(), at(dx=-1), first=True)
        w_send(3, 6, member(), at(dc=1), first=True)

    def b_pass():
        wc[3, 0].wait_recv()
        w_send(3, 4, member(-1), at(dx=1))
        w_send(3, 7, member(-1), at(dc=1))
        wc[3, 1].wait_recv()
        w_send(3, 8, member(1), at(dc=1))

    def b_last():
        wc[3, 4].wait_recv()
        w_send(3, 9, member(2), at(dc=1))

    tok_send(0, 0, 0)
    tok_send(1, 0, 0)
    tok_send(0, 0, 1)
    tok_send(1, 0, 1)
    b_first()
    w_first(0)
    local = [pltpu.make_async_copy(tokens, stage, loc.at[0]),
             pltpu.make_async_copy(enc, enc_all.at[member()], loc.at[1]),
             pltpu.make_async_copy(dec, dec_all.at[member()], loc.at[2]),
             pltpu.make_async_copy(bias, bias_all.at[member()], loc.at[3])]
    for copy in local:
        copy.start()

    ids = lax.broadcasted_iota(jnp.int32, (blocks, rows), 0)
    hits = [act[pl.ds(k, 1), :] == ids for k in range(4)]
    named = (hits[0] | hits[1]) | (hits[2] | hits[3])
    before = (lax.broadcasted_iota(jnp.int32, (rows, rows), 0)
              < lax.broadcasted_iota(jnp.int32, (rows, rows), 1))
    rank = jnp.dot(jnp.where(named, 1.0, 0.0).astype(BF), jnp.where(before, 1.0, 0.0).astype(BF),
                   preferred_element_type=F32)
    where_to = rank + table[...]
    for k in range(4):
        tgt[0, pl.ds(k, 1), :] = jnp.sum(jnp.where(hits[k], where_to, 0.0), axis=0, keepdims=True)
    tgt[0, pl.ds(4, 4), :] = jnp.full((4, rows), -1.0, F32)
    tgt_send(0, 0)
    tgt_send(1, 0)

    base = (z * slots).astype(F32)

    def gather(ref, i, buf):
        def pick(j, carry):
            n = slots // 4
            r0 = pl.multiple_of(j * n, n)
            place = (lax.broadcasted_iota(jnp.int32, (n, rows), 0) + r0).astype(F32) + base
            t = tgt[i]
            hit = ((t[0:1] == place) | (t[1:2] == place)) | ((t[2:3] == place) | (t[3:4] == place))
            picks[pl.ds(r0, n), :] = jnp.where(hit, 1.0, 0.0).astype(BF)
            return carry

        lax.fori_loop(0, 4, pick, 0)
        def product(j, carry):
            for t in range(4):
                n = width // 8
                cs = pl.ds(pl.multiple_of((j * 4 + t) * n, n), n)
                got = jnp.dot(picks[...], ref[:, cs], preferred_element_type=F32)
                work[buf, :, cs] = (got - dbias[:, cs]).astype(BF)
            return carry

        lax.fori_loop(0, 2, product, 0)

    def encode(i, n):
        def one(j, carry):
            for b in range(8):
                r0 = pl.multiple_of((j * 8 + b) * PAD, PAD)
                got = jnp.dot(work[0:n, pl.ds(r0, PAD), :].reshape(n * PAD, width),
                              enc_all[j * 2 + b // 4, :, pl.ds(b % 4 * 128, 128)], preferred_element_type=F32)
                for t in range(n):
                    preact[i + t, pl.ds(r0, PAD), :] = got[t * PAD:(t + 1) * PAD]
            return carry

        lax.fori_loop(0, 4, one, 0)

    def load(i, dst, k):
        copy = pltpu.make_async_copy(tokbuf.at[i - 1], dst, loc.at[k])
        copy.start()
        return copy

    ysum, ycode = {}, {}

    def y_start(g, i, n):
        for o in range(1, 4):
            to = pl.multiple_of(((y + o) % 4) * quarter, quarter)
            ysum[g, o] = send(preact.at[pl.ds(i, n), pl.ds(to, quarter)], parts_in.at[o - 1, pl.ds(i, n)],
                              ys_s.at[g, o - 1], ys_r.at[g, o - 1], at(dy=o))
            sent.append(ysum[g, o])

    mine = pl.multiple_of(y * quarter, quarter)

    def y_codes(g, i, n):
        for o in range(1, 4):
            ysum[g, o].wait_recv()
        per = bias_all[pl.ds(2 * y, 2)].reshape(quarter // PAD, 1, 128)
        for j in range(i, i + n):
            total = preact[j, pl.ds(mine, quarter), :] + parts_in[0, j] + parts_in[1, j] + parts_in[2, j]
            total = total.reshape(quarter // PAD, PAD, 128) + per
            codes[j, pl.ds(mine, quarter), :] = jnp.maximum(total, 0.0).astype(BF).reshape(quarter, 128)
        for o in range(1, 4):
            view = codes.at[pl.ds(i, n), pl.ds(mine, quarter)]
            ycode[g, o] = send(view, view, yc_s.at[g, o - 1], yc_r.at[g, o - 1], at(dy=o))
            sent.append(ycode[g, o])

    def y_done(g):
        for o in range(1, 4):
            ycode[g, o].wait_recv()

    def tok_pass(k, o):
        for d in range(2):
            tok[d, k, o].wait_recv()
            if k < 2 or o == 0:
                tok_send(d, k + 1, o)

    def tgt_pass(k):
        for d in range(2):
            tg[d, k].wait_recv()
            if k < 2 or d == 0:
                tgt_send(d, k + 1)

    def decode(i, buf, q):
        cs = pl.ds(q * side, side)

        def one(m, carry):
            for b in range(4):
                r0 = pl.multiple_of((m * 4 + b) * PAD, PAD)
                work[buf, pl.ds(r0, PAD), cs] = jnp.dot(
                    codes[i, pl.ds(r0, PAD), :], dec_all[m, pl.ds(b * 128, 128), cs],
                    preferred_element_type=F32).astype(BF)
            return carry

        lax.fori_loop(0, 8, one, 0)

    def spread(i, h):
        t = jnp.concatenate([tgt[i], jnp.zeros((120, rows), F32)], axis=0)
        cols = jnp.transpose(t)[h * half:(h + 1) * half]
        place = lax.broadcasted_iota(jnp.int32, (half, slots), 1).astype(F32) + base
        hit = (((cols[:, 0:1] == place) | (cols[:, 1:2] == place))
               | ((cols[:, 2:3] == place) | (cols[:, 3:4] == place)))
        return jnp.where(hit, 1.0, 0.0).astype(BF)

    def tiles(q):
        n = side // 2
        return [pl.ds(q * side + j * n, n) for j in range(2)]

    def sums(h, buf, q, plus):
        for cs in tiles(q):
            total = jnp.dot(sels[h], work[buf, :, cs], preferred_element_type=F32)
            for ref in plus:
                total = total + ref[:, cs].astype(F32)
            yield cs, total

    def combine(h, buf, q, dst, plus=()):
        for cs, total in sums(h, buf, q, plus):
            dst[:, cs] = total.astype(BF)

    rs = {}

    def rs_send(d, q, k, o, src):
        cs = pl.ds(q * side, side)
        rs[d, q, k, o] = send(src.at[:, cs], rs_in.at[d, k, o, :, cs], rs_s.at[d, q, k, o], rs_r.at[d, q, k, o],
                              at(dz=1 if d == 0 else -1))
        if k > 1 or (k == 1 and o == 0):
            sent.append(rs[d, q, k, o])

    def decode_two(i, q):
        def one(d, carry):
            decode(i - d, d, q)
            return carry

        lax.fori_loop(0, 2, one, 0)

    def near_first(q):
        decode_two(6, q)
        for d in range(2):
            sels[1 - d] = spread(6 - d, 1 - d)
            combine(1 - d, d, q, rs_first.at[d, 1])
            rs_send(d, q, 1, 1, rs_first.at[d, 1])

    def far_first(q):
        decode(7, 0, q)
        for d in range(2):
            sels[d] = spread(7, d)
            combine(d, 0, q, rs_first.at[d, 0])
            rs_send(d, q, 0, 0, rs_first.at[d, 0])

    def ring_step(q, k, o):
        decode_two(8 - 2 * k, q)
        for d in range(2):
            got = rs_in.at[d, k - 1, o]
            h = o if d == 0 else 1 - o
            sels[h] = spread(8 - 2 * k - d, h)
            rs[d, q, k - 1, o].wait_recv()
            combine(h, d, q, got, (got,))
            rs_send(d, q, k, o, got)

    def ring_sum(q):
        decode(0, 0, q)
        for d in range(2):
            rs[d, q, 0, 0].wait_send()
            rs[d, q, 1, 1].wait_send()
            sels[d] = spread(0, d)
        for d in range(2):
            h = 1 - d
            rs[d, q, 3, 1].wait_recv()
            for cs, total in sums(h, 0, q, (rs_in.at[d, 3, 1], dbias)):
                top = total.astype(BF)
                rs_first[0, h, :, cs] = top
                rs_first[1, h, :, cs] = (total - top.astype(F32)).astype(BF)

    def ring_end(q):
        for d in range(2):
            rs[d, q, 3, 0].wait_recv()
            for cs in tiles(q):
                total = rs_first[0, d, :, cs].astype(F32) + rs_first[1, d, :, cs].astype(F32)
                out[pl.ds(d * half, half), cs] = (total + rs_in[d, 3, 0, :, cs].astype(F32)).astype(BF)

    b_pass()
    tok_pass(0, 0)
    w_pass(0)
    w_first(1)
    tok_pass(0, 1)
    tgt_pass(0)
    one = load(1, out, 5)
    for copy in local:
        copy.wait()
    gather(stage, 0, 0)
    two = load(2, stage, 4)
    one.wait()
    gather(out, 1, 1)
    w_mid(0)
    b_last()
    tok_pass(1, 0)
    tok_pass(1, 1)
    tgt_pass(1)
    three = load(3, out, 5)
    w_last(0)
    w_done(3, (6, 7, 8, 9))
    w_done(0, (6, 7, 8, 9, 10))
    encode(0, 2)
    y_start(0, 0, 2)
    w_pass(1)
    w_first(2)
    two.wait()
    gather(stage, 2, 0)
    four = load(4, stage, 4)
    three.wait()
    gather(out, 3, 1)
    encode(2, 2)
    tok_pass(2, 0)
    four.wait()
    gather(stage, 4, 0)
    encode(4, 1)
    y_start(1, 2, 3)
    y_codes(0, 0, 2)
    w_mid(1)
    tok_pass(2, 1)
    tgt_pass(2)
    five, six = load(5, stage, 4), load(6, out, 5)
    w_last(1)
    five.wait()
    gather(stage, 5, 0)
    six.wait()
    gather(out, 6, 1)
    encode(5, 2)
    y_start(2, 5, 2)
    y_codes(1, 2, 3)
    y_codes(2, 5, 2)
    w_done(1, (6, 7, 8, 9, 10))
    for g in range(3):
        y_done(g)
    near_first(0)
    w_pass(2)
    tg[0, 3].wait_recv()
    tok[0, 3, 0].wait_recv()
    tok[1, 3, 0].wait_recv()
    gather(last, 7, 0)
    encode(7, 1)
    y_start(3, 7, 1)
    w_mid(2)
    y_codes(3, 7, 1)
    ring_step(0, 2, 1)
    y_done(3)
    far_first(0)
    w_last(2)
    ring_step(0, 3, 1)
    w_done(2, (6, 7, 8, 9, 10))
    near_first(1)
    far_first(1)
    ring_step(0, 1, 0)
    ring_step(1, 2, 1)
    ring_step(1, 1, 0)
    ring_step(0, 2, 0)
    ring_step(1, 3, 1)
    ring_step(1, 2, 0)
    ring_sum(0)
    ring_step(0, 3, 0)
    ring_sum(1)
    ring_step(1, 3, 0)
    ring_end(0)
    ring_end(1)
    for copy in sent:
        copy.wait_send()


def local(tokens, active, placement_map, enc_weight, enc_bias, dec_weight, dec_bias):
    rows, width = tokens.shape
    blocks = placement_map.shape[0]
    slots = blocks // NZ * PAD
    depth = enc_weight.shape[1]
    p = placement_map
    table = ((p // 8) % NZ * slots + (p // (8 * NZ) * 8 + p % 8) * PAD).astype(F32).reshape(blocks, 1)
    vmem, hbm = pl.BlockSpec(memory_space=pltpu.VMEM), pl.BlockSpec(memory_space=pl.ANY)
    half = rows // 2
    dma = pltpu.SemaphoreType.DMA
    out, _ = pl.pallas_call(
        kernel,
        out_shape=(jax.ShapeDtypeStruct((rows, width), BF), jax.ShapeDtypeStruct((6, rows, width), BF)),
        in_specs=[hbm, vmem, vmem, hbm, vmem, hbm, vmem],
        out_specs=(vmem, hbm),
        scratch_shapes=[
            pltpu.VMEM((8, width, depth), BF),
            pltpu.VMEM((8, depth, width), BF),
            pltpu.VMEM((8, 4, 128), F32),
            pltpu.VMEM((8, 8, rows), F32),
            pltpu.VMEM((rows, width), BF),
            pltpu.VMEM((rows, width), BF),
            pltpu.VMEM((2, slots, width), BF),
            pltpu.VMEM((slots, rows), BF),
            pltpu.VMEM((8, slots, 128), F32),
            pltpu.VMEM((3, 8, slots // 4, 128), F32),
            pltpu.VMEM((8, slots, 128), BF),
            pltpu.VMEM((2, half, slots), BF),
            pltpu.VMEM((2, 2, half, width), BF),
            pltpu.VMEM((2, 4, 2, half, width), BF),
            dma((2, 4, 2)), dma((2, 4, 2)),
            dma((2, 4)), dma((2, 4)),
            dma((4, 11)), dma((4, 11)),
            dma((4, 3)), dma((4, 3)),
            dma((4, 3)), dma((4, 3)),
            dma((2, 2, 4, 2)), dma((2, 2, 4, 2)),
            dma((6,)),
        ],
        compiler_params=pltpu.CompilerParams(collective_id=0, has_side_effects=True, vmem_limit_bytes=63 << 20),
        name="encode_decode",
    )(tokens, active.T, table, enc_weight, enc_bias.reshape(4, 128), dec_weight, dec_bias.reshape(1, width))
    return out


def solution(mesh):
    return jax.shard_map(
        local,
        mesh=mesh,
        in_specs=(
            P(("seq", "lat"), "tp"),
            P(("seq", "lat"), None),
            P(),
            P("tp", ("seq", "lat")),
            P(("seq", "lat")),
            P(("seq", "lat"), "tp"),
            P("tp"),
        ),
        out_specs=P(("seq", "lat"), "tp"),
        check_vma=False,
    )
```

```python
import jax
import jax.numpy as jnp
from jax import lax
from jax.experimental import pallas as pl
from jax.experimental.pallas import tpu as pltpu
from jax.sharding import PartitionSpec as P

NX, NZ = 4, 8
PAD = 16
MESH = pl.DeviceIdType.MESH
BF, F32 = jnp.bfloat16, jnp.float32


def kernel(tokens, act, table, enc, bias, dec, dbias, out, tokbuf,
           enc_all, dec_all, bias_all, tgt, stage, last, work, picks, preact, parts_in, codes, sels,
           rs_first, rs_in,
           tok_s, tok_r, tgt_s, tgt_r, w_s, w_r, ys_s, ys_r, yc_s, yc_r, rs_s, rs_r, loc):
    rows, width = tokens.shape
    half = rows // 2
    blocks = table.shape[0]
    row_blocks = blocks // NZ
    slots = row_blocks * PAD
    quarter = slots // 4
    s, y, c = lax.axis_index("seq"), lax.axis_index("tp"), lax.axis_index("lat")
    x, z = s // NZ, s % NZ

    def at(dx=0, dz=0, dy=0, dc=0):
        return (((x + dx + NX) % NX) * NZ + (z + dz + NZ) % NZ, (y + dy) % 4, (c + dc) % 2)

    def member(dx=0, dc=0):
        return ((x + dx + NX) % NX) * 2 + (c + dc) % 2

    def send(src, dst, ss, rs, dev):
        copy = pltpu.make_async_remote_copy(src_ref=src, dst_ref=dst, send_sem=ss, recv_sem=rs,
                                            device_id=dev, device_id_type=MESH)
        copy.start()
        return copy

    sent = []
    peers = [at(dz=1), at(dz=-1), at(dx=1), at(dx=-1), at(dc=1), at(dy=1), at(dy=2), at(dy=3)]
    barrier = pltpu.get_barrier_semaphore()
    for dev in peers:
        pl.semaphore_signal(barrier, inc=1, device_id=dev, device_id_type=MESH)
    pl.semaphore_wait(barrier, len(peers))

    def part(ref, h):
        return ref.at[pl.ds(h * half, half)]

    tok = {}

    def tok_send(d, k, o):
        h = o if d == 0 else 1 - o
        src = tokens if k == 0 else tokbuf.at[2 * k - 2 + d]
        dst = last if k == 3 else tokbuf.at[2 * k + d]
        tok[d, k, o] = send(part(src, h), part(dst, h), tok_s.at[d, k, o], tok_r.at[d, k, o],
                            at(dz=1 if d == 0 else -1))
        sent.append(tok[d, k, o])

    tg = {}

    def tgt_send(d, k):
        src = 0 if k == 0 else 2 * k - 1 + d
        dst = 7 if k == 3 else 2 * k + 1 + d
        tg[d, k] = send(tgt.at[src], tgt.at[dst], tgt_s.at[d, k], tgt_r.at[d, k], at(dz=1 if d == 0 else -1))
        sent.append(tg[d, k])

    wc = {}
    store = (enc_all, dec_all, dec_all, bias_all)
    own = (enc, dec, dec, bias)
    side = width // 2

    def w_send(kind, slot, m, dev, first=False, piece=None):
        dst = store[kind].at[m]
        src = own[kind] if first else dst
        n = src.shape[0] if piece is None else src.shape[0] // 2
        rs_ = pl.ds(0 if piece is None else piece * n, n)
        if kind in (1, 2):
            cs = pl.ds((kind - 1) * side, side)
            src, dst = src.at[rs_, cs], dst.at[rs_, cs]
        elif kind == 0:
            src, dst = src.at[rs_], dst.at[rs_]
        wc[kind, slot] = send(src, dst, w_s.at[kind, slot], w_r.at[kind, slot], dev)
        sent.append(wc[kind, slot])

    def w_first(kind):
        for p in range(2):
            w_send(kind, p, member(), at(dx=1), first=True, piece=p)
            w_send(kind, 3 - p, member(), at(dx=-1), first=True, piece=1 - p)
        w_send(kind, 6, member(), at(dc=1), first=True)

    def w_pass(kind):
        wc[kind, 0].wait_recv()
        w_send(kind, 4, member(-1), at(dx=1), piece=0)
        wc[kind, 3].wait_recv()
        w_send(kind, 5, member(1), at(dx=-1), piece=1)

    def w_mid(kind):
        wc[kind, 1].wait_recv()
        w_send(kind, 7, member(-1), at(dc=1))
        wc[kind, 2].wait_recv()
        w_send(kind, 8, member(1), at(dc=1))

    def w_last(kind):
        for p in range(2):
            wc[kind, 4 + p].wait_recv()
            w_send(kind, 9 + p, member(2), at(dc=1), piece=p)

    def w_done(kind, slots):
        for slot in slots:
            wc[kind, slot].wait_recv()

    def b_first():
        w_send(3, 0, member(), at(dx=1), first=True)
        w_send(3, 1, member(), at(dx=-1), first=True)
        w_send(3, 6, member(), at(dc=1), first=True)

    def b_pass():
        wc[3, 0].wait_recv()
        w_send(3, 4, member(-1), at(dx=1))
        w_send(3, 7, member(-1), at(dc=1))
        wc[3, 1].wait_recv()
        w_send(3, 8, member(1), at(dc=1))

    def b_last():
        wc[3, 4].wait_recv()
        w_send(3, 9, member(2), at(dc=1))

    tok_send(0, 0, 0)
    tok_send(1, 0, 0)
    tok_send(0, 0, 1)
    tok_send(1, 0, 1)
    b_first()
    w_first(0)
    local = [pltpu.make_async_copy(tokens, stage, loc.at[0]),
             pltpu.make_async_copy(enc, enc_all.at[member()], loc.at[1]),
             pltpu.make_async_copy(dec, dec_all.at[member()], loc.at[2]),
             pltpu.make_async_copy(bias, bias_all.at[member()], loc.at[3])]
    for copy in local:
        copy.start()

    ids = lax.broadcasted_iota(jnp.int32, (blocks, rows), 0)
    hits = [act[pl.ds(k, 1), :] == ids for k in range(4)]
    named = (hits[0] | hits[1]) | (hits[2] | hits[3])
    before = (lax.broadcasted_iota(jnp.int32, (rows, rows), 0)
              < lax.broadcasted_iota(jnp.int32, (rows, rows), 1))
    rank = jnp.dot(jnp.where(named, 1.0, 0.0).astype(BF), jnp.where(before, 1.0, 0.0).astype(BF),
                   preferred_element_type=F32)
    where_to = rank + table[...]
    for k in range(4):
        tgt[0, pl.ds(k, 1), :] = jnp.sum(jnp.where(hits[k], where_to, 0.0), axis=0, keepdims=True)
    tgt[0, pl.ds(4, 4), :] = jnp.full((4, rows), -1.0, F32)
    tgt_send(0, 0)
    tgt_send(1, 0)

    base = (z * slots).astype(F32)

    def gather(ref, i, buf):
        def pick(j, carry):
            n = slots // 4
            r0 = pl.multiple_of(j * n, n)
            place = (lax.broadcasted_iota(jnp.int32, (n, rows), 0) + r0).astype(F32) + base
            t = tgt[i]
            hit = ((t[0:1] == place) | (t[1:2] == place)) | ((t[2:3] == place) | (t[3:4] == place))
            picks[pl.ds(r0, n), :] = jnp.where(hit, 1.0, 0.0).astype(BF)
            return carry

        lax.fori_loop(0, 4, pick, 0)
        def product(j, carry):
            for t in range(4):
                n = width // 8
                cs = pl.ds(pl.multiple_of((j * 4 + t) * n, n), n)
                got = jnp.dot(picks[...], ref[:, cs], preferred_element_type=F32)
                work[buf, :, cs] = (got - dbias[:, cs]).astype(BF)
            return carry

        lax.fori_loop(0, 2, product, 0)

    def encode(i, n):
        def one(j, carry):
            for b in range(8):
                r0 = pl.multiple_of((j * 8 + b) * PAD, PAD)
                got = jnp.dot(work[0:n, pl.ds(r0, PAD), :].reshape(n * PAD, width),
                              enc_all[j * 2 + b // 4, :, pl.ds(b % 4 * 128, 128)], preferred_element_type=F32)
                for t in range(n):
                    preact[i + t, pl.ds(r0, PAD), :] = got[t * PAD:(t + 1) * PAD]
            return carry

        lax.fori_loop(0, 4, one, 0)

    def load(i, dst, k):
        copy = pltpu.make_async_copy(tokbuf.at[i - 1], dst, loc.at[k])
        copy.start()
        return copy

    ysum, ycode = {}, {}

    def y_start(g, i, n):
        for o in range(1, 4):
            to = pl.multiple_of(((y + o) % 4) * quarter, quarter)
            ysum[g, o] = send(preact.at[pl.ds(i, n), pl.ds(to, quarter)], parts_in.at[o - 1, pl.ds(i, n)],
                              ys_s.at[g, o - 1], ys_r.at[g, o - 1], at(dy=o))
            sent.append(ysum[g, o])

    mine = pl.multiple_of(y * quarter, quarter)

    def y_codes(g, i, n):
        for o in range(1, 4):
            ysum[g, o].wait_recv()
        per = bias_all[pl.ds(2 * y, 2)].reshape(quarter // PAD, 1, 128)
        for j in range(i, i + n):
            total = preact[j, pl.ds(mine, quarter), :] + parts_in[0, j] + parts_in[1, j] + parts_in[2, j]
            total = total.reshape(quarter // PAD, PAD, 128) + per
            codes[j, pl.ds(mine, quarter), :] = jnp.maximum(total, 0.0).astype(BF).reshape(quarter, 128)
        for o in range(1, 4):
            view = codes.at[pl.ds(i, n), pl.ds(mine, quarter)]
            ycode[g, o] = send(view, view, yc_s.at[g, o - 1], yc_r.at[g, o - 1], at(dy=o))
            sent.append(ycode[g, o])

    def y_done(g):
        for o in range(1, 4):
            ycode[g, o].wait_recv()

    def tok_pass(k, o):
        for d in range(2):
            tok[d, k, o].wait_recv()
            if k < 2 or o == 0:
                tok_send(d, k + 1, o)

    def tgt_pass(k):
        for d in range(2):
            tg[d, k].wait_recv()
            if k < 2 or d == 0:
                tgt_send(d, k + 1)

    def decode(i, buf, q):
        cs = pl.ds(q * side, side)

        def one(m, carry):
            for b in range(4):
                r0 = pl.multiple_of((m * 4 + b) * PAD, PAD)
                work[buf, pl.ds(r0, PAD), cs] = jnp.dot(
                    codes[i, pl.ds(r0, PAD), :], dec_all[m, pl.ds(b * 128, 128), cs],
                    preferred_element_type=F32).astype(BF)
            return carry

        lax.fori_loop(0, 8, one, 0)

    def spread(i, h):
        t = jnp.concatenate([tgt[i], jnp.zeros((120, rows), F32)], axis=0)
        cols = jnp.transpose(t)[h * half:(h + 1) * half]
        place = lax.broadcasted_iota(jnp.int32, (half, slots), 1).astype(F32) + base
        hit = (((cols[:, 0:1] == place) | (cols[:, 1:2] == place))
               | ((cols[:, 2:3] == place) | (cols[:, 3:4] == place)))
        return jnp.where(hit, 1.0, 0.0).astype(BF)

    def tiles(q):
        n = side // 2
        return [pl.ds(q * side + j * n, n) for j in range(2)]

    def sums(h, buf, q, plus):
        for cs in tiles(q):
            total = jnp.dot(sels[h], work[buf, :, cs], preferred_element_type=F32)
            for ref in plus:
                total = total + ref[:, cs].astype(F32)
            yield cs, total

    def combine(h, buf, q, dst, plus=()):
        for cs, total in sums(h, buf, q, plus):
            dst[:, cs] = total.astype(BF)

    rs = {}

    def rs_send(d, q, k, o, src):
        cs = pl.ds(q * side, side)
        rs[d, q, k, o] = send(src.at[:, cs], rs_in.at[d, k, o, :, cs], rs_s.at[d, q, k, o], rs_r.at[d, q, k, o],
                              at(dz=1 if d == 0 else -1))
        if k > 1 or (k == 1 and o == 0):
            sent.append(rs[d, q, k, o])

    def decode_two(i, q):
        def one(d, carry):
            decode(i - d, d, q)
            return carry

        lax.fori_loop(0, 2, one, 0)

    def near_first(q):
        decode_two(6, q)
        for d in range(2):
            sels[1 - d] = spread(6 - d, 1 - d)
            combine(1 - d, d, q, rs_first.at[d, 1])
            rs_send(d, q, 1, 1, rs_first.at[d, 1])

    def far_first(q):
        decode(7, 0, q)
        for d in range(2):
            sels[d] = spread(7, d)
            combine(d, 0, q, rs_first.at[d, 0])
            rs_send(d, q, 0, 0, rs_first.at[d, 0])

    def ring_step(q, k, o):
        decode_two(8 - 2 * k, q)
        for d in range(2):
            got = rs_in.at[d, k - 1, o]
            h = o if d == 0 else 1 - o
            sels[h] = spread(8 - 2 * k - d, h)
            rs[d, q, k - 1, o].wait_recv()
            combine(h, d, q, got, (got,))
            rs_send(d, q, k, o, got)

    def ring_sum(q):
        decode(0, 0, q)
        for d in range(2):
            rs[d, q, 0, 0].wait_send()
            rs[d, q, 1, 1].wait_send()
            sels[d] = spread(0, d)
        for d in range(2):
            h = 1 - d
            rs[d, q, 3, 1].wait_recv()
            for cs, total in sums(h, 0, q, (rs_in.at[d, 3, 1], dbias)):
                top = total.astype(BF)
                rs_first[0, h, :, cs] = top
                rs_first[1, h, :, cs] = (total - top.astype(F32)).astype(BF)

    def ring_end(q):
        for d in range(2):
            rs[d, q, 3, 0].wait_recv()
            for cs in tiles(q):
                total = rs_first[0, d, :, cs].astype(F32) + rs_first[1, d, :, cs].astype(F32)
                out[pl.ds(d * half, half), cs] = (total + rs_in[d, 3, 0, :, cs].astype(F32)).astype(BF)

    b_pass()
    tok_pass(0, 0)
    w_pass(0)
    w_first(1)
    tok_pass(0, 1)
    tgt_pass(0)
    one = load(1, out, 5)
    for copy in local:
        copy.wait()
    gather(stage, 0, 0)
    two = load(2, stage, 4)
    one.wait()
    gather(out, 1, 1)
    w_mid(0)
    b_last()
    tok_pass(1, 0)
    tok_pass(1, 1)
    tgt_pass(1)
    three = load(3, out, 5)
    w_last(0)
    w_done(3, (6, 7, 8, 9))
    w_done(0, (6, 7, 8, 9, 10))
    encode(0, 2)
    y_start(0, 0, 2)
    w_pass(1)
    w_first(2)
    two.wait()
    gather(stage, 2, 0)
    four = load(4, stage, 4)
    three.wait()
    gather(out, 3, 1)
    encode(2, 2)
    tok_pass(2, 0)
    four.wait()
    gather(stage, 4, 0)
    encode(4, 1)
    y_start(1, 2, 3)
    y_codes(0, 0, 2)
    w_mid(1)
    tok_pass(2, 1)
    tgt_pass(2)
    five, six = load(5, stage, 4), load(6, out, 5)
    w_last(1)
    five.wait()
    gather(stage, 5, 0)
    six.wait()
    gather(out, 6, 1)
    encode(5, 2)
    y_start(2, 5, 2)
    y_codes(1, 2, 3)
    y_codes(2, 5, 2)
    w_done(1, (6, 7, 8, 9, 10))
    for g in range(3):
        y_done(g)
    near_first(0)
    w_pass(2)
    tg[0, 3].wait_recv()
    tok[0, 3, 0].wait_recv()
    tok[1, 3, 0].wait_recv()
    gather(last, 7, 0)
    encode(7, 1)
    y_start(3, 7, 1)
    w_mid(2)
    y_codes(3, 7, 1)
    y_done(3)
    far_first(0)
    ring_step(0, 2, 1)
    w_last(2)
    ring_step(0, 3, 1)
    w_done(2, (6, 7, 8, 9, 10))
    near_first(1)
    far_first(1)
    ring_step(0, 1, 0)
    ring_step(1, 2, 1)
    ring_step(1, 1, 0)
    ring_step(0, 2, 0)
    ring_step(1, 3, 1)
    ring_step(1, 2, 0)
    ring_sum(0)
    ring_step(0, 3, 0)
    ring_sum(1)
    ring_step(1, 3, 0)
    ring_end(0)
    ring_end(1)
    for copy in sent:
        copy.wait_send()


def local(tokens, active, placement_map, enc_weight, enc_bias, dec_weight, dec_bias):
    rows, width = tokens.shape
    blocks = placement_map.shape[0]
    slots = blocks // NZ * PAD
    depth = enc_weight.shape[1]
    p = placement_map
    table = ((p // 8) % NZ * slots + (p // (8 * NZ) * 8 + p % 8) * PAD).astype(F32).reshape(blocks, 1)
    vmem, hbm = pl.BlockSpec(memory_space=pltpu.VMEM), pl.BlockSpec(memory_space=pl.ANY)
    half = rows // 2
    dma = pltpu.SemaphoreType.DMA
    out, _ = pl.pallas_call(
        kernel,
        out_shape=(jax.ShapeDtypeStruct((rows, width), BF), jax.ShapeDtypeStruct((6, rows, width), BF)),
        in_specs=[hbm, vmem, vmem, hbm, vmem, hbm, vmem],
        out_specs=(vmem, hbm),
        scratch_shapes=[
            pltpu.VMEM((8, width, depth), BF),
            pltpu.VMEM((8, depth, width), BF),
            pltpu.VMEM((8, 4, 128), F32),
            pltpu.VMEM((8, 8, rows), F32),
            pltpu.VMEM((rows, width), BF),
            pltpu.VMEM((rows, width), BF),
            pltpu.VMEM((2, slots, width), BF),
            pltpu.VMEM((slots, rows), BF),
            pltpu.VMEM((8, slots, 128), F32),
            pltpu.VMEM((3, 8, slots // 4, 128), F32),
            pltpu.VMEM((8, slots, 128), BF),
            pltpu.VMEM((2, half, slots), BF),
            pltpu.VMEM((2, 2, half, width), BF),
            pltpu.VMEM((2, 4, 2, half, width), BF),
            dma((2, 4, 2)), dma((2, 4, 2)),
            dma((2, 4)), dma((2, 4)),
            dma((4, 11)), dma((4, 11)),
            dma((4, 3)), dma((4, 3)),
            dma((4, 3)), dma((4, 3)),
            dma((2, 2, 4, 2)), dma((2, 2, 4, 2)),
            dma((6,)),
        ],
        compiler_params=pltpu.CompilerParams(collective_id=0, has_side_effects=True, vmem_limit_bytes=63 << 20),
        name="encode_decode",
    )(tokens, active.T, table, enc_weight, enc_bias.reshape(4, 128), dec_weight, dec_bias.reshape(1, width))
    return out


def solution(mesh):
    return jax.shard_map(
        local,
        mesh=mesh,
        in_specs=(
            P(("seq", "lat"), "tp"),
            P(("seq", "lat"), None),
            P(),
            P("tp", ("seq", "lat")),
            P(("seq", "lat")),
            P(("seq", "lat"), "tp"),
            P("tp"),
        ),
        out_specs=P(("seq", "lat"), "tp"),
        check_vma=False,
    )
```
